32 devices in a mesh: groups: 2 (over y), cells: 4 (over z), sub: 2 (over x), rep: 2 (over core).
Axes of the slice: x: 2, y: 2, z: 4, core: 2. Of those that a mesh axis runs over, the one named last changes fastest.
Arguments:
- queries: bfloat16 [128, 1024], P('groups', 'sub'), parts along dimension 0, may hold values from -6 to 6
- rerank_queries: bfloat16 [128, 1024], P(('groups', 'cells', 'rep'), 'sub'), parts along dimension 0, may hold values from -6 to 6
- coarse_book: bfloat16 [64, 256, 16], P('sub'), may hold values from -0.1875 to 0.1875
- refine_book: bfloat16 [16, 256, 64], P('sub'), may hold values from -0.1875 to 0.1875
- coarse_codes: int32 [64, 65536], P('sub', ('groups', 'cells')), parts along dimension 1, may hold values from 0 to 255
- refine_codes: int32 [16, 65536], P('sub', ('groups', 'cells')), parts along dimension 1, may hold values from 0 to 255
- block_place: int32 [512], P('groups'), parts along dimension 0, may hold values from 0 to 255, as said below
- candidates: int32 [128, 4], P(('groups', 'cells', 'rep')), parts along dimension 0, may hold values from 0 to 255, as said below
Outputs:
- coarse_scores: bfloat16 [128, 4, 8192], P(('groups', 'cells', 'rep'), None, 'sub'), parts along dimension 0
- refined: bfloat16 [128, 4, 128], P(('groups', 'cells', 'rep'), 'sub'), parts along dimension 0
The draws below stay inside these ranges and needn't reach their ends.
There are 2 independent parts, one for each index of `groups`. The reference program is written for one: setup_inputs(seed, part) draws one part's arguments, and reference() takes and returns one part's arrays. A program takes and returns all parts, laid end to end along the dimension named above; an argument that names none is the same for every part. Nothing has to cross between parts.
Inputs may be any that keep to these rules, and one draw needn't show every extreme that they name: `block_place`: A permutation: every block id has one storage position. `candidates`: take the aligned blocks of 8 query rows (one query owner's rows). Of the 32 candidate blocks of such rows, at most 24 have block_place // 64 equal to any one value; in every draw some value is reached by exactly 24 from every such block of rows.
All inputs are finite; a program needn't handle non-finite values.
Results may differ from the reference program's by a relative error of at most 0.0049.
Values may be sent and summed in bfloat16 or wider, within the bound.
No kernel may reach another device: no remote copies, remote signals or barrier semaphores. Data moves between devices by JAX's collectives and lax.ppermute only.
A program may use at most 64 MiB of HBM per device.

```python
from functools import partial
import jax
import jax.numpy as jnp
from jax import lax

D = 1024
MC = 64
MR = 16
KC = 256
BLOCK = 128
NC = 4
NQ_OWN = 8
ITEMS_DEV = 8192
HOLDERS = 4
OWNERS = 8
NQ = 64
ITEMS = 32768
BLOCKS_DEV = 64
NBLOCKS = 256
CAP = 24


def place_table(key):
    return jax.random.permutation(jax.random.fold_in(key, 101), NBLOCKS).astype(jnp.int32)


def draw_block_place(key, part):
    return place_table(key)


def owner_holders(busiest, owner_key):
    request_count = NQ_OWN * NC
    spread = (jnp.arange(HOLDERS - 1, dtype=jnp.int32) + busiest + 1) % HOLDERS
    reservoir = jnp.repeat(spread, CAP)
    picked = jax.random.permutation(jax.random.fold_in(owner_key, 1), reservoir)[:request_count - CAP]
    listing = jnp.concatenate([jnp.full((CAP,), busiest, jnp.int32), picked.astype(jnp.int32)])
    return jax.random.permutation(jax.random.fold_in(owner_key, 2), listing)


def draw_candidates(key, part):
    storage = place_table(key)
    ordering = jnp.argsort(storage, stable=True).astype(jnp.int32)
    busiest = jax.random.randint(jax.random.fold_in(key, 202), (), 0, HOLDERS, dtype=jnp.int32)
    owner_keys = jax.random.split(jax.random.fold_in(key, 303), OWNERS)
    holder = jax.vmap(partial(owner_holders, busiest))(owner_keys)
    within = jax.random.randint(jax.random.fold_in(key, 404), (OWNERS, NQ_OWN * NC), 0, BLOCKS_DEV, dtype=jnp.int32)
    blocks = jnp.take(ordering, holder * BLOCKS_DEV + within, axis=0)
    return blocks.reshape(OWNERS * NQ_OWN, NC).astype(jnp.int32)


def place_ends(values, own_key, smallest, largest):
    index_at = [jax.random.randint(jax.random.fold_in(own_key, axis), (), 0, length) for axis, length in enumerate(values.shape)]
    longest = values.shape.index(max(values.shape))
    beside = index_at[:longest] + [(index_at[longest] + 1) % values.shape[longest]] + index_at[longest + 1:]
    return values.at[tuple(index_at)].set(smallest).at[tuple(beside)].set(largest)


def block_levels(rng, dims, cuts, smallest, largest):
    factor_of, own = 1.0, jax.random.fold_in(rng, 6)
    for axis_at, shards_of in cuts:
        heights = jnp.exp(jax.random.uniform(jax.random.fold_in(own, axis_at), (shards_of,), jnp.float32, smallest / len(cuts), largest / len(cuts)))
        factor_of = factor_of * jnp.repeat(heights, dims[axis_at] // shards_of).reshape([-1 if axis == axis_at else 1 for axis in range(len(dims))])
    return factor_of


def centred(rng, extent, scale, bound, shards=(), kind=jnp.bfloat16):
    level = block_levels(rng, extent, shards, -0.22, 0.18) if shards else 1.0
    drawn = jax.random.normal(rng, extent, jnp.float32) * scale * level
    return jnp.minimum(jnp.maximum(drawn, -bound), bound).astype(kind)


def setup_inputs(seed: int = 0, part: int = 0) -> dict:
    seeds = jax.random.split(jax.random.key(seed), 9)
    part_keys = jax.random.split(jax.random.fold_in(seeds[8], part), 9)
    return {
        "queries": centred(part_keys[0], (NQ, D), 1.0, 6.0, ((1, 2),)),
        "rerank_queries": centred(part_keys[1], (NQ, D), 1.0, 6.0, ((0, 8), (1, 2))),
        "coarse_book": centred(seeds[2], (MC, KC, D // MC), D ** -0.5, 0.1875, ((0, 2),)),
        "refine_book": centred(seeds[3], (MR, KC, D // MR), D ** -0.5, 0.1875, ((0, 2),)),
        "coarse_codes": place_ends(jax.random.randint(part_keys[4], (MC, ITEMS), 0, KC), jax.random.fold_in(part_keys[4], 1), 0, KC - 1).astype(jnp.int32),
        "refine_codes": place_ends(jax.random.randint(part_keys[5], (MR, ITEMS), 0, KC), jax.random.fold_in(part_keys[5], 1), 0, KC - 1).astype(jnp.int32),
        "block_place": draw_block_place(jax.random.fold_in(jax.random.fold_in(seeds[8], part), 71), part),
        "candidates": draw_candidates(jax.random.fold_in(jax.random.fold_in(seeds[8], part), 71), part),
    }


def reference(queries, rerank_queries, coarse_book, refine_book, coarse_codes, refine_codes, block_place, candidates):
    query_count = queries.shape[0]
    coarse_rows = queries.astype(jnp.float32).reshape(query_count, MC, D // MC)
    coarse_lookup = jnp.einsum("qmd,mkd->qmk", coarse_rows, coarse_book.astype(jnp.float32)).astype(jnp.bfloat16)

    def add_coarse(subspace, running):
        lookup = lax.dynamic_index_in_dim(coarse_lookup, subspace, 1, keepdims=False)
        column = lax.dynamic_index_in_dim(coarse_codes, subspace, 0, keepdims=False)
        return running + jnp.take(lookup, column, axis=1).astype(jnp.float32)

    coarse_sum = lax.fori_loop(0, MC, add_coarse, jnp.zeros((query_count, coarse_codes.shape[1]), jnp.float32))
    coarse_scores = coarse_sum.astype(jnp.bfloat16).reshape(query_count, HOLDERS, ITEMS_DEV)

    refine_rows = rerank_queries.astype(jnp.float32).reshape(query_count, MR, D // MR)
    refine_lookup = jnp.einsum("qmd,mkd->qmk", refine_rows, refine_book.astype(jnp.float32)).astype(jnp.bfloat16)
    position = jnp.take(block_place, candidates, axis=0).astype(jnp.int32)
    offsets = jnp.arange(BLOCK, dtype=jnp.int32)
    tiles = (position[:, :, None] * BLOCK + offsets[None, None, :]).reshape(query_count, NC * BLOCK).astype(jnp.int32)
    picked = jnp.take_along_axis(coarse_sum, tiles, axis=1)

    def add_refine(subspace, running):
        lookup = lax.dynamic_index_in_dim(refine_lookup, subspace, 1, keepdims=False)
        column = lax.dynamic_index_in_dim(refine_codes, subspace, 0, keepdims=False)
        chosen = jnp.take(column, tiles, axis=0)
        return running + jnp.take_along_axis(lookup, chosen, axis=1).astype(jnp.float32)

    summed = lax.fori_loop(0, MR, add_refine, picked)
    refined = summed.astype(jnp.bfloat16).reshape(query_count, NC, BLOCK)
    return coarse_scores, refined
```

```python
from functools import partial

import jax
import jax.numpy as jnp
from jax import lax
from jax.experimental import pallas as pl
from jax.experimental.pallas import tpu as pltpu
from jax.sharding import PartitionSpec as P

BLOCK = 128
LANES = 128

ALONG_LANES = lax.GatherDimensionNumbers(
    offset_dims=(),
    collapsed_slice_dims=(1,),
    start_index_map=(1,),
    operand_batching_dims=(0,),
    start_indices_batching_dims=(0,),
)


def take_lanes(table, index):
    return lax.gather(
        table,
        index[..., None],
        ALONG_LANES,
        (1, 1),
        mode=lax.GatherScatterMode.PROMISE_IN_BOUNDS,
    )


def lookup(table, codes):
    within = codes & (LANES - 1)
    found = take_lanes(table[:, :LANES], within)
    for start in range(LANES, table.shape[1], LANES):
        found = jnp.where(codes >= start, take_lanes(table[:, start : start + LANES], within), found)
    return found


def coarse_kernel(shift, chunk, q_ref, book_ref, codes_ref, *refs):
    out_refs, tiles_ref = refs[:-1], refs[-1]
    spaces, depth, _ = book_ref.shape
    holders, own, part = out_refs[0].shape
    half = lax.axis_index("rep")
    start = (lax.axis_index("sub") ^ shift) * part
    halves = q_ref.shape[0] // holders
    rows = jnp.concatenate(
        [q_ref[h * halves + half].astype(jnp.float32) for h in range(holders)], axis=0
    ).astype(jnp.bfloat16)

    for first in range(0, part, chunk):

        def fill(group, _):
            lane = pl.multiple_of(group * LANES, LANES)
            at = pl.multiple_of(start + first + lane, LANES)
            for m in range(spaces):
                table = book_ref[m].astype(jnp.float32)
                codes = jnp.broadcast_to(codes_ref[m : m + 1, pl.ds(at, LANES)], (8, LANES))
                found = [lookup(table[d : d + 8], codes) for d in range(0, depth, 8)]
                tiles_ref[m * depth : (m + 1) * depth, pl.ds(lane, LANES)] = jnp.concatenate(
                    found, axis=0
                ).astype(jnp.bfloat16)
            return 0

        lax.fori_loop(0, chunk // LANES, fill, 0, unroll=2)
        scores = jnp.dot(rows, tiles_ref[...], preferred_element_type=jnp.float32)
        for h in range(holders):
            for out_ref in out_refs:
                out_ref[h, :, first : first + chunk] = scores[h * own : (h + 1) * own].astype(
                    out_ref.dtype
                )


def coarse_part(shift, parts, holders, own, queries, book, codes):
    part = codes.shape[1] // parts
    chunk = min(part, 2048)
    kinds = (jnp.float32, jnp.bfloat16) if shift else (jnp.float32,)
    return pl.pallas_call(
        partial(coarse_kernel, shift, chunk),
        out_shape=tuple(jax.ShapeDtypeStruct((holders, own, part), k) for k in kinds),
        scratch_shapes=[pltpu.VMEM((book.shape[0] * book.shape[1], chunk), jnp.bfloat16)],
        name="coarse_%d" % shift,
    )(queries, book, codes)


def refine_kernel(parts, holders, *refs):
    place_ref = refs[0]
    cand_refs = refs[1 : 1 + holders]
    rerank_refs = refs[1 + holders : 1 + 2 * holders]
    book_ref, codes_ref = refs[1 + 2 * holders : 3 + 2 * holders]
    part_refs = refs[3 + 2 * holders : 3 + 2 * holders + parts]
    out_ref, wide_ref, table_ref = refs[3 + 2 * holders + parts :]
    per_query, own = cand_refs[0].shape
    spaces, cell_stored = codes_ref.shape
    width = book_ref.shape[0]
    depth = width // spaces
    cell_blocks = cell_stored // BLOCK
    part_blocks = cell_blocks // parts
    cell = lax.axis_index("cells")
    sub = lax.axis_index("sub")
    slot = -(-spaces // 8) * 8
    mine = lax.broadcasted_iota(jnp.int32, (slot, width), 1) // depth == (
        lax.broadcasted_iota(jnp.int32, (slot, width), 0)
    )
    for k in range(holders):
        rerank = rerank_refs[k][...].astype(jnp.float32)
        for j in range(own):
            at = (k * own + j) * slot
            wide_ref[at : at + slot, :] = jnp.where(mine, rerank[j : j + 1], 0.0)
    table_ref[...] = jnp.dot(
        wide_ref[...].astype(jnp.bfloat16), book_ref[...], preferred_element_type=jnp.float32
    )
    row = lax.broadcasted_iota(jnp.int32, (own, BLOCK), 0)
    for k in range(holders):
        owner = cell ^ k

        def query(j, kept):
            kept = list(kept)
            table = table_ref[pl.ds(pl.multiple_of((k * own + j) * slot, slot), slot), :][:spaces]
            for c in range(per_query):
                position = place_ref[cand_refs[k][c, j]]
                here = position // cell_blocks == cell
                block = position % cell_blocks
                lanes = pl.ds(pl.multiple_of(block * BLOCK, BLOCK), BLOCK)
                found = lookup(table, codes_ref[:, lanes])
                shift = (block // part_blocks) ^ sub
                within = pl.ds(pl.multiple_of(block % part_blocks * BLOCK, BLOCK), BLOCK)
                coarse = part_refs[0][owner, :, within]
                for other in range(1, parts):
                    coarse = jnp.where(shift == other, part_refs[other][owner, :, within], coarse)
                coarse = jnp.where(row == j, coarse, 0.0)
                if spaces == own:
                    total = jnp.sum(found + coarse, axis=0, keepdims=True)
                else:
                    total = jnp.sum(found, axis=0, keepdims=True) + jnp.sum(
                        coarse, axis=0, keepdims=True
                    )
                kept[c] = jnp.where((row == j) & here, total, kept[c])
            return tuple(kept)

        empty = (jnp.zeros((own, BLOCK), jnp.float32),) * per_query
        for c, value in enumerate(lax.fori_loop(0, own, query, empty, unroll=2)):
            out_ref[k, :, c * BLOCK : (c + 1) * BLOCK] = value


def refine_partials(parts, holders, place, cands, reranks, book, codes, scores):
    per_query, own = cands[0].shape
    rows = holders * own * (-(-codes.shape[0] // 8) * 8)
    smem = pl.BlockSpec(memory_space=pltpu.SMEM)
    vmem = pl.BlockSpec(memory_space=pltpu.VMEM)
    return pl.pallas_call(
        partial(refine_kernel, parts, holders),
        in_specs=[smem] * (1 + holders) + [vmem] * (holders + 2 + parts),
        out_shape=jax.ShapeDtypeStruct((holders, own, per_query * BLOCK), jnp.float32),
        scratch_shapes=[
            pltpu.VMEM((rows, book.shape[0]), jnp.float32),
            pltpu.VMEM((rows, book.shape[1]), jnp.float32),
        ],
        name="refine",
    )(place, *cands, *reranks, book, codes, *scores)


def combine_kernel(parts, fine_ref, *refs):
    part_refs, out_refs = refs[:parts], refs[parts:]
    cell = lax.axis_index("cells")
    part = part_refs[0].shape[2]
    for k, out_ref in enumerate(out_refs):
        total = part_refs[0][cell ^ k]
        for other_ref in part_refs[1:]:
            total = total + other_ref[cell ^ k].astype(jnp.float32)
        out_ref[:, :part] = total.astype(jnp.bfloat16)
        out_ref[:, part:] = fine_ref[k].astype(jnp.bfloat16)


def combine(fine, parts):
    holders, own, part = parts[0].shape
    shape = jax.ShapeDtypeStruct((own, part + fine.shape[2]), jnp.bfloat16)
    return pl.pallas_call(
        partial(combine_kernel, len(parts)), out_shape=(shape,) * holders, name="combine"
    )(fine, *parts)


def fine_sum_kernel(subs, width, *refs):
    in_refs, out_refs = refs[:-subs], refs[-subs:]
    own = in_refs[0].shape[0]
    part = in_refs[0].shape[1] - subs * width
    sub = lax.axis_index("sub")
    total = in_refs[0][:, part:].astype(jnp.float32)
    for in_ref in in_refs[1:]:
        total = total + in_ref[:, part:].astype(jnp.float32)
    for shift, out_ref in enumerate(out_refs):
        value = total[:, :width]
        for other in range(1, subs):
            value = jnp.where(sub ^ shift == other, total[:, other * width : (other + 1) * width], value)
        out_ref[...] = value


def fine_sum(subs, width, got):
    own = got[0].shape[0]
    shape = jax.ShapeDtypeStruct((own, width), jnp.float32)
    return pl.pallas_call(
        partial(fine_sum_kernel, subs, width), out_shape=(shape,) * subs, name="fine_sum"
    )(*got)


def arrange_kernel(*refs):
    in_refs, out_ref, order_ref = refs[:-2], refs[-2], refs[-1]
    cell = lax.axis_index("cells")
    part = out_ref.shape[2]
    for k, in_ref in enumerate(in_refs):
        order_ref[cell ^ k] = in_ref[:, :part].astype(jnp.float32)
    out_ref[...] = jnp.stack([order_ref[h] for h in range(len(in_refs))], axis=1).astype(
        jnp.bfloat16
    )


def arrange(part, got):
    holders, own = len(got), got[0].shape[0]
    return pl.pallas_call(
        arrange_kernel,
        out_shape=jax.ShapeDtypeStruct((own, holders, part), jnp.bfloat16),
        scratch_shapes=[pltpu.VMEM((holders, own, part), jnp.float32)],
        name="arrange",
    )(*got)


def swap(value, axis, shift):
    return lax.ppermute(value, axis, [(i, i ^ shift) for i in range(lax.axis_size(axis))])


def shards(
    queries,
    rerank_queries,
    coarse_book,
    refine_book,
    coarse_codes,
    refine_codes,
    block_place,
    candidates,
):
    holders = lax.axis_size("cells")
    subs = lax.axis_size("sub")
    own, features = rerank_queries.shape
    per_query = candidates.shape[1]
    part = coarse_codes.shape[1] // subs
    cands = [candidates.T]
    reranks = [rerank_queries]
    for k in range(1, holders):
        reranks.append(swap(rerank_queries, "cells", k))
        cands.append(swap(candidates.T, "cells", k))
    rows = queries.reshape(queries.shape[0] // own, own, features)
    book = jnp.swapaxes(coarse_book, 1, 2)
    fine_book = jnp.swapaxes(refine_book, 1, 2).reshape(features, refine_book.shape[1])
    scores, sums = [], []
    for shift in range(1, subs):
        score, sent = coarse_part(shift, subs, holders, own, rows, book, coarse_codes)
        scores.append(score)
        sums.append(swap(sent, "sub", shift))
    (score,) = coarse_part(0, subs, holders, own, rows, book, coarse_codes)
    scores.insert(0, score)
    fine = refine_partials(
        subs, holders, block_place, cands, reranks, fine_book, refine_codes, scores
    )
    pieces = combine(fine, [score] + sums)
    got = [pieces[0]] + [swap(pieces[k], "cells", k) for k in range(1, holders)]
    width = per_query // subs * BLOCK
    fine_parts = fine_sum(subs, width, got)
    refined = fine_parts[0]
    for shift in range(1, subs):
        refined = refined + swap(fine_parts[shift], "sub", shift)
    coarse = arrange(part, got)
    return coarse, refined.astype(jnp.bfloat16).reshape(own, per_query // subs, BLOCK)


def solution(mesh):
    placed = (
        P("groups", "sub"),
        P(("groups", "cells", "rep"), "sub"),
        P("sub", None, None),
        P("sub", None, None),
        P("sub", ("groups", "cells")),
        P("sub", ("groups", "cells")),
        P("groups"),
        P(("groups", "cells", "rep"), None),
    )
    return jax.shard_map(
        shards,
        mesh=mesh,
        in_specs=placed,
        out_specs=(
            P(("groups", "cells", "rep"), None, "sub"),
            P(("groups", "cells", "rep"), "sub", None),
        ),
        check_vma=False,
    )
```

```python
from functools import partial

import jax
import jax.numpy as jnp
from jax import lax
from jax.experimental import pallas as pl
from jax.experimental.pallas import tpu as pltpu
from jax.sharding import PartitionSpec as P


BLOCK = 128
LANES = 128

ALONG_LANES = lax.GatherDimensionNumbers(
    offset_dims=(),
    collapsed_slice_dims=(1,),
    start_index_map=(1,),
    operand_batching_dims=(0,),
    start_indices_batching_dims=(0,),
)


def take_lanes(table, index):
    return lax.gather(
        table,
        index[..., None],
        ALONG_LANES,
        (1, 1),
        mode=lax.GatherScatterMode.PROMISE_IN_BOUNDS,
    )


def lookup(table, codes):
    within = codes & (LANES - 1)
    found = take_lanes(table[:, :LANES], within)
    for start in range(LANES, table.shape[1], LANES):
        found = jnp.where(codes >= start, take_lanes(table[:, start : start + LANES], within), found)
    return found


def on_chip(value):
    return pltpu.with_memory_space_constraint(value, pltpu.VMEM)


def coarse_kernel(halves, q_ref, book_ref, codes_ref, *refs):
    out_refs, tiles_ref = refs[:halves], refs[halves]
    spaces, depth, _ = book_ref.shape
    holders, own, chunk = out_refs[0].shape
    half = lax.axis_index("rep")
    rows = jnp.concatenate(
        [
            q_ref[h * halves + (half ^ r)].astype(jnp.float32)
            for r in range(halves)
            for h in range(holders)
        ],
        axis=0,
    ).astype(jnp.bfloat16)

    def fill(group, _):
        lanes = pl.ds(pl.multiple_of(group * LANES, LANES), LANES)
        for m in range(spaces):
            table = book_ref[m].astype(jnp.float32)
            codes = jnp.broadcast_to(codes_ref[m : m + 1, lanes], (8, LANES))
            found = [lookup(table[d : d + 8], codes) for d in range(0, depth, 8)]
            tiles_ref[m * depth : (m + 1) * depth, lanes] = jnp.concatenate(found, axis=0).astype(
                jnp.bfloat16
            )
        return 0

    lax.fori_loop(0, chunk // LANES, fill, 0, unroll=2)
    scores = jnp.dot(rows, tiles_ref[...], preferred_element_type=jnp.float32)
    for r in range(halves):
        for h in range(holders):
            at = (r * holders + h) * own
            out_refs[r][h] = scores[at : at + own].astype(out_refs[r].dtype)


def coarse_part(shift, subs, halves, holders, own, queries, book, codes):
    spaces, stored = codes.shape
    quarter = stored // subs // halves

    def place(step):
        return 0, (lax.axis_index("sub") ^ shift) * halves + lax.axis_index("rep")

    whole = pl.BlockSpec(memory_space=pltpu.VMEM)
    kinds = [jnp.bfloat16] * halves
    if shift == 0:
        kinds[0] = jnp.float32
    return pl.pallas_call(
        partial(coarse_kernel, halves),
        grid=(1,),
        in_specs=[whole, whole, pl.BlockSpec((spaces, quarter), place)],
        out_specs=[whole] * halves,
        out_shape=[pltpu.VMEM((holders, own, quarter), kind) for kind in kinds],
        scratch_shapes=[pltpu.VMEM((book.shape[0] * book.shape[1], quarter), jnp.bfloat16)],
    )(queries, book, codes)


def refine_kernel(holders, place_ref, cand_ref, rerank_ref, book_ref, *refs):
    codes_refs = refs[:holders]
    out_ref, wide_ref, table_ref = refs[holders:]
    per_query, own = cand_ref.shape
    spaces, stored = codes_refs[0].shape
    width = book_ref.shape[0]
    depth = width // spaces
    cell_blocks = stored // BLOCK
    cell = lax.axis_index("cells")
    slot = -(-spaces // 8) * 8
    mine = lax.broadcasted_iota(jnp.int32, (slot, width), 1) // depth == (
        lax.broadcasted_iota(jnp.int32, (slot, width), 0)
    )
    rerank = rerank_ref[...].astype(jnp.float32)
    for j in range(own):
        wide_ref[j * slot : (j + 1) * slot, :] = jnp.where(mine, rerank[j : j + 1], 0.0)
    table_ref[...] = jnp.dot(
        wide_ref[...].astype(jnp.bfloat16), book_ref[...], preferred_element_type=jnp.float32
    )
    for j in range(own):
        table = table_ref[j * slot : j * slot + spaces, :]
        for c in range(per_query):
            position = place_ref[cand_ref[c, j]]
            source = position // cell_blocks ^ cell
            lanes = pl.ds(pl.multiple_of(position % cell_blocks * BLOCK, BLOCK), BLOCK)
            codes = codes_refs[0][:, lanes].astype(jnp.float32)
            for k in range(1, holders):
                codes = jnp.where(source == k, codes_refs[k][:, lanes].astype(jnp.float32), codes)
            found = lookup(table, codes.astype(jnp.int32))
            out_ref[j : j + 1, c * BLOCK : (c + 1) * BLOCK] = jnp.sum(found, axis=0, keepdims=True)


def refine_partials(place, cands, reranks, book, codes):
    per_query, own = cands.shape
    spaces = codes[0].shape[0]
    rows = own * (-(-spaces // 8) * 8)
    smem = pl.BlockSpec(memory_space=pltpu.SMEM)
    vmem = pl.BlockSpec(memory_space=pltpu.VMEM)
    return pl.pallas_call(
        partial(refine_kernel, len(codes)),
        in_specs=[smem, smem] + [vmem] * (2 + len(codes)),
        out_specs=vmem,
        out_shape=pltpu.VMEM((own, per_query * BLOCK), jnp.float32),
        scratch_shapes=[
            pltpu.VMEM((rows, book.shape[0]), jnp.float32),
            pltpu.VMEM((rows, book.shape[1]), jnp.float32),
        ],
        name="refine",
    )(place, cands, reranks, book, *[on_chip(c) for c in codes])


def combine_kernel(subs, halves, *refs):
    in_refs, out_refs = refs[: subs * halves], refs[subs * halves :]
    cell = lax.axis_index("cells")
    quarter = in_refs[0].shape[2]
    for k, out_ref in enumerate(out_refs):
        for r in range(halves):
            total = in_refs[r][cell ^ k].astype(jnp.float32)
            for shift in range(1, subs):
                total = total + in_refs[shift * halves + r][cell ^ k].astype(jnp.float32)
            at = pl.multiple_of((lax.axis_index("rep") ^ r) * quarter, quarter)
            out_ref[:, pl.ds(at, quarter)] = total.astype(jnp.bfloat16)


def combine(subs, halves, sums):
    holders, own, quarter = sums[0].shape
    vmem = pl.BlockSpec(memory_space=pltpu.VMEM)
    return pl.pallas_call(
        partial(combine_kernel, subs, halves),
        in_specs=[vmem] * len(sums),
        out_specs=[vmem] * holders,
        out_shape=[pltpu.VMEM((own, quarter * halves), jnp.bfloat16)] * holders,
        name="combine",
    )(*[on_chip(s) for s in sums])


def pick_kernel(subs, holders, place_ref, cand_ref, fine_ref, *refs):
    got_refs, out_refs = refs[:holders], refs[holders:]
    per_query, own = cand_ref.shape
    part_blocks = got_refs[0].shape[1] // BLOCK
    cell_blocks = part_blocks * subs
    cell = lax.axis_index("cells")
    sub = lax.axis_index("sub")
    row = lax.broadcasted_iota(jnp.int32, (own, BLOCK), 0)
    sums = []
    for c in range(per_query):
        total = jnp.zeros((own, BLOCK), jnp.float32)
        for j in range(own):
            position = place_ref[cand_ref[c, j]]
            block = position % cell_blocks
            source = position // cell_blocks ^ cell
            lanes = pl.ds(pl.multiple_of(block % part_blocks * BLOCK, BLOCK), BLOCK)
            score = got_refs[0][:, lanes].astype(jnp.float32)
            for k in range(1, holders):
                score = jnp.where(source == k, got_refs[k][:, lanes].astype(jnp.float32), score)
            total = jnp.where((row == j) & (block // part_blocks == sub), score, total)
        sums.append(total + fine_ref[:, c * BLOCK : (c + 1) * BLOCK])
    each = per_query // subs
    for shift, out_ref in enumerate(out_refs):
        for c in range(each):
            value = sums[c]
            for other in range(1, subs):
                value = jnp.where(sub ^ shift == other, sums[other * each + c], value)
            out_ref[:, c * BLOCK : (c + 1) * BLOCK] = value


def pick(subs, place, cands, fine, got):
    per_query, own = cands.shape
    smem = pl.BlockSpec(memory_space=pltpu.SMEM)
    vmem = pl.BlockSpec(memory_space=pltpu.VMEM)
    return pl.pallas_call(
        partial(pick_kernel, subs, len(got)),
        in_specs=[smem, smem] + [vmem] * (1 + len(got)),
        out_specs=[vmem] * subs,
        out_shape=[pltpu.VMEM((own, per_query // subs * BLOCK), jnp.float32)] * subs,
        name="pick",
    )(place, cands, on_chip(fine), *[on_chip(g) for g in got])


def arrange_kernel(*refs):
    in_refs, out_ref, order_ref = refs[:-2], refs[-2], refs[-1]
    cell = lax.axis_index("cells")
    for k, in_ref in enumerate(in_refs):
        order_ref[cell ^ k] = in_ref[...].astype(jnp.float32)
    out_ref[...] = jnp.stack([order_ref[h] for h in range(len(in_refs))], axis=1).astype(
        jnp.bfloat16
    )


def arrange(got):
    holders, (own, part) = len(got), got[0].shape
    return pl.pallas_call(
        arrange_kernel,
        out_shape=jax.ShapeDtypeStruct((own, holders, part), jnp.bfloat16),
        scratch_shapes=[pltpu.VMEM((holders, own, part), jnp.float32)],
        name="arrange",
    )(*[on_chip(g) for g in got])


def swap(value, axis, shift):
    return lax.ppermute(value, axis, [(i, i ^ shift) for i in range(lax.axis_size(axis))])


def shards(
    queries,
    rerank_queries,
    coarse_book,
    refine_book,
    coarse_codes,
    refine_codes,
    block_place,
    candidates,
):
    holders = lax.axis_size("cells")
    subs = lax.axis_size("sub")
    halves = lax.axis_size("rep")
    own, features = rerank_queries.shape
    per_query = candidates.shape[1]
    rows = queries.reshape(queries.shape[0] // own, own, features)
    book = jnp.swapaxes(coarse_book, 1, 2)
    fine_book = jnp.swapaxes(refine_book, 1, 2).reshape(features, refine_book.shape[1])
    sums = []
    for shift in [*range(1, subs), 0]:
        sent = coarse_part(shift, subs, halves, holders, own, rows, book, coarse_codes)
        if shift:
            rows, sent = lax.optimization_barrier((rows, sent))
        here = []
        for r, value in enumerate(sent):
            if shift or r:
                value = swap(value, ("sub", "rep"), shift * halves + r)
            here.append(value)
        sums = sums + here if shift else here + sums
    fine_codes = [refine_codes.astype(jnp.bfloat16)]
    for k in range(1, holders):
        fine_codes.append(swap(fine_codes[0], "cells", k))
    fine = refine_partials(block_place, candidates.T, rerank_queries, fine_book, fine_codes)
    pieces = combine(subs, halves, sums)
    got = [pieces[0]]
    for k in range(1, holders):
        got.append(swap(pieces[k], "cells", k))
    fine_parts = pick(subs, block_place, candidates.T, fine, got)
    refined = fine_parts[0]
    for shift in range(1, subs):
        refined = refined + swap(fine_parts[shift], "sub", shift)
    coarse = arrange(got)
    return coarse, refined.astype(jnp.bfloat16).reshape(own, per_query // subs, BLOCK)


def solution(mesh):
    placed = (
        P("groups", "sub"),
        P(("groups", "cells", "rep"), "sub"),
        P("sub", None, None),
        P("sub", None, None),
        P("sub", ("groups", "cells")),
        P("sub", ("groups", "cells")),
        P("groups"),
        P(("groups", "cells", "rep"), None),
    )
    return jax.shard_map(
        shards,
        mesh=mesh,
        in_specs=placed,
        out_specs=(
            P(("groups", "cells", "rep"), None, "sub"),
            P(("groups", "cells", "rep"), "sub", None),
        ),
        check_vma=False,
    )
```

```python
from functools import partial

import jax
import jax.numpy as jnp
from jax import lax
from jax.experimental import pallas as pl
from jax.experimental.pallas import tpu as pltpu
from jax.sharding import PartitionSpec as P


BLOCK = 128
LANES = 128

ALONG_LANES = lax.GatherDimensionNumbers(
    offset_dims=(),
    collapsed_slice_dims=(1,),
    start_index_map=(1,),
    operand_batching_dims=(0,),
    start_indices_batching_dims=(0,),
)


def take_lanes(table, index):
    return lax.gather(
        table,
        index[..., None],
        ALONG_LANES,
        (1, 1),
        mode=lax.GatherScatterMode.PROMISE_IN_BOUNDS,
    )


def lookup(table, codes):
    within = codes & (LANES - 1)
    found = take_lanes(table[:, :LANES], within)
    for start in range(LANES, table.shape[1], LANES):
        found = jnp.where(codes >= start, take_lanes(table[:, start : start + LANES], within), found)
    return found


def on_chip(value):
    return pltpu.with_memory_space_constraint(value, pltpu.VMEM)


def decode(table, codes):
    codes = jnp.broadcast_to(codes.astype(jnp.int16), (table.shape[0], codes.shape[1]))
    within = codes & jnp.int16(LANES - 1)
    found = take_lanes(table[:, :LANES], within)
    for start in range(LANES, table.shape[1], LANES):
        found = jnp.where(
            codes >= jnp.int16(start), take_lanes(table[:, start : start + LANES], within), found
        )
    return found


def coarse_kernel(halves, q_ref, book_ref, codes_ref, out_ref):
    spaces, depth, _ = book_ref.shape
    _, own, tiles = out_ref.shape
    holders = out_ref.shape[0] // halves
    half = lax.axis_index("rep")
    rows = jnp.concatenate(
        [
            q_ref[h * halves + (half ^ r)].astype(jnp.float32)
            for r in range(halves)
            for h in range(holders)
        ],
        axis=0,
    ).astype(jnp.bfloat16)
    step = min(spaces, 256 // depth)
    for first in range(0, tiles, 2 * LANES):
        scores = None
        for low in range(0, spaces, step):
            decoded = jnp.concatenate(
                [
                    jnp.concatenate(
                        [
                            decode(book_ref[m], codes_ref[m : m + 1, at : at + LANES])
                            for at in (first, first + LANES)
                        ],
                        axis=1,
                    )
                    for m in range(low, low + step)
                ],
                axis=0,
            )
            part = jnp.dot(
                rows[:, low * depth : (low + step) * depth],
                decoded,
                preferred_element_type=jnp.float32,
            )
            scores = part if scores is None else scores + part
        for h in range(halves * holders):
            out_ref[h, :, first : first + 2 * LANES] = scores[h * own : (h + 1) * own].astype(
                out_ref.dtype
            )


def coarse_part(shift, subs, halves, holders, own, queries, book, codes):
    spaces, stored = codes.shape
    quarter = stored // subs // halves

    def place(step):
        return 0, (lax.axis_index("sub") ^ shift) * halves + lax.axis_index("rep")

    whole = pl.BlockSpec(memory_space=pltpu.VMEM)
    return pl.pallas_call(
        partial(coarse_kernel, halves),
        grid=(1,),
        in_specs=[whole, whole, pl.BlockSpec((spaces, quarter), place)],
        out_specs=whole,
        out_shape=pltpu.VMEM(
            (halves * holders, own, quarter), jnp.bfloat16 if shift else jnp.float32
        ),
    )(queries, book, codes)


def refine_kernel(holders, place_ref, cand_ref, rerank_ref, book_ref, *refs):
    codes_refs = refs[:holders]
    out_ref, wide_ref, table_ref = refs[holders:]
    per_query, own = cand_ref.shape
    spaces, stored = codes_refs[0].shape
    width = book_ref.shape[0]
    depth = width // spaces
    cell_blocks = stored // BLOCK
    cell = lax.axis_index("cells")
    slot = -(-spaces // 8) * 8
    mine = lax.broadcasted_iota(jnp.int32, (slot, width), 1) // depth == (
        lax.broadcasted_iota(jnp.int32, (slot, width), 0)
    )
    rerank = rerank_ref[...].astype(jnp.float32)
    for j in range(own):
        wide_ref[j * slot : (j + 1) * slot, :] = jnp.where(mine, rerank[j : j + 1], 0.0)
    table_ref[...] = jnp.dot(
        wide_ref[...].astype(jnp.bfloat16), book_ref[...], preferred_element_type=jnp.float32
    )
    for j in range(own):
        table = table_ref[j * slot : j * slot + spaces, :]
        for c in range(per_query):
            position = place_ref[cand_ref[c, j]]
            source = lax.div(position, cell_blocks) ^ cell
            lanes = pl.ds(pl.multiple_of(lax.rem(position, cell_blocks) * BLOCK, BLOCK), BLOCK)
            codes = codes_refs[0][:, lanes].astype(jnp.float32)
            for k in range(1, holders):
                codes = jnp.where(source == k, codes_refs[k][:, lanes].astype(jnp.float32), codes)
            found = lookup(table, codes.astype(jnp.int32))
            out_ref[j : j + 1, c * BLOCK : (c + 1) * BLOCK] = jnp.sum(found, axis=0, keepdims=True)


def refine_partials(place, cands, reranks, book, codes):
    per_query, own = cands.shape
    spaces = codes[0].shape[0]
    rows = own * (-(-spaces // 8) * 8)
    smem = pl.BlockSpec(memory_space=pltpu.SMEM)
    vmem = pl.BlockSpec(memory_space=pltpu.VMEM)
    return pl.pallas_call(
        partial(refine_kernel, len(codes)),
        in_specs=[smem, smem] + [vmem] * (2 + len(codes)),
        out_specs=vmem,
        out_shape=pltpu.VMEM((own, per_query * BLOCK), jnp.float32),
        scratch_shapes=[
            pltpu.VMEM((rows, book.shape[0]), jnp.float32),
            pltpu.VMEM((rows, book.shape[1]), jnp.float32),
        ],
        name="refine",
    )(place, cands, reranks, book, *[on_chip(c) for c in codes])


def reduce_kernel(halves, *refs):
    in_refs, out_refs = refs[:-halves], refs[-halves:]
    holders = out_refs[0].shape[0]
    for r, out_ref in enumerate(out_refs):
        for h in range(holders):
            total = in_refs[0][r * holders + h]
            for in_ref in in_refs[1:]:
                total = total + in_ref[r * holders + h].astype(jnp.float32)
            out_ref[h] = total.astype(jnp.bfloat16)


def reduce_subs(halves, sums):
    rows, own, quarter = sums[0].shape
    vmem = pl.BlockSpec(memory_space=pltpu.VMEM)
    return pl.pallas_call(
        partial(reduce_kernel, halves),
        in_specs=[vmem] * len(sums),
        out_specs=[vmem] * halves,
        out_shape=[pltpu.VMEM((rows // halves, own, quarter), jnp.bfloat16)] * halves,
        name="reduce",
    )(*[on_chip(s) for s in sums])


def combine_kernel(halves, *refs):
    in_refs, out_refs = refs[:halves], refs[halves:]
    cell = lax.axis_index("cells")
    quarter = in_refs[0].shape[2]
    for k, out_ref in enumerate(out_refs):
        for r, in_ref in enumerate(in_refs):
            at = pl.multiple_of((lax.axis_index("rep") ^ r) * quarter, quarter)
            out_ref[:, pl.ds(at, quarter)] = in_ref[cell ^ k]


def combine(quarters):
    holders, own, quarter = quarters[0].shape
    vmem = pl.BlockSpec(memory_space=pltpu.VMEM)
    return pl.pallas_call(
        partial(combine_kernel, len(quarters)),
        in_specs=[vmem] * len(quarters),
        out_specs=[vmem] * holders,
        out_shape=[pltpu.VMEM((own, quarter * len(quarters)), jnp.bfloat16)] * holders,
        name="combine",
    )(*[on_chip(q) for q in quarters])


def pick_kernel(subs, holders, place_ref, cand_ref, fine_ref, *refs):
    got_refs, out_refs = refs[:holders], refs[holders:]
    per_query, own = cand_ref.shape
    part_blocks = got_refs[0].shape[1] // BLOCK
    cell_blocks = part_blocks * subs
    cell = lax.axis_index("cells")
    sub = lax.axis_index("sub")
    row = lax.broadcasted_iota(jnp.int32, (own, BLOCK), 0)
    sums = []
    for c in range(per_query):
        total = jnp.zeros((own, BLOCK), jnp.float32)
        for j in range(own):
            position = place_ref[cand_ref[c, j]]
            block = lax.rem(position, cell_blocks)
            source = lax.div(position, cell_blocks) ^ cell
            lanes = pl.ds(pl.multiple_of(lax.rem(block, part_blocks) * BLOCK, BLOCK), BLOCK)
            score = got_refs[0][:, lanes].astype(jnp.float32)
            for k in range(1, holders):
                score = jnp.where(source == k, got_refs[k][:, lanes].astype(jnp.float32), score)
            total = jnp.where((row == j) & (lax.div(block, part_blocks) == sub), score, total)
        sums.append(total + fine_ref[:, c * BLOCK : (c + 1) * BLOCK])
    each = per_query // subs
    for shift, out_ref in enumerate(out_refs):
        for c in range(each):
            value = sums[c]
            for other in range(1, subs):
                value = jnp.where(sub ^ shift == other, sums[other * each + c], value)
            out_ref[:, c * BLOCK : (c + 1) * BLOCK] = value


def pick(subs, place, cands, fine, got):
    per_query, own = cands.shape
    smem = pl.BlockSpec(memory_space=pltpu.SMEM)
    vmem = pl.BlockSpec(memory_space=pltpu.VMEM)
    return pl.pallas_call(
        partial(pick_kernel, subs, len(got)),
        in_specs=[smem, smem] + [vmem] * (1 + len(got)),
        out_specs=[vmem] * subs,
        out_shape=[pltpu.VMEM((own, per_query // subs * BLOCK), jnp.float32)] * subs,
        name="pick",
    )(place, cands, on_chip(fine), *[on_chip(g) for g in got])


def arrange_kernel(*refs):
    in_refs, out_ref, order_ref = refs[:-2], refs[-2], refs[-1]
    cell = lax.axis_index("cells")
    for k, in_ref in enumerate(in_refs):
        order_ref[cell ^ k] = in_ref[...].astype(jnp.float32)
    out_ref[...] = jnp.stack([order_ref[h] for h in range(len(in_refs))], axis=1).astype(
        jnp.bfloat16
    )


def arrange(got):
    holders, (own, part) = len(got), got[0].shape
    return pl.pallas_call(
        arrange_kernel,
        out_shape=jax.ShapeDtypeStruct((own, holders, part), jnp.bfloat16),
        scratch_shapes=[pltpu.VMEM((holders, own, part), jnp.float32)],
        name="arrange",
    )(*[on_chip(g) for g in got])


def finish_kernel(*refs):
    in_refs, out_ref = refs[:-1], refs[-1]
    total = in_refs[0][...]
    for in_ref in in_refs[1:]:
        total = total + in_ref[...]
    out_ref[...] = jnp.stack(
        [total[:, c * BLOCK : (c + 1) * BLOCK] for c in range(out_ref.shape[1])], axis=1
    ).astype(jnp.bfloat16)


def finish(parts):
    own, width = parts[0].shape
    return pl.pallas_call(
        finish_kernel,
        out_shape=jax.ShapeDtypeStruct((own, width // BLOCK, BLOCK), jnp.bfloat16),
        name="finish",
    )(*[on_chip(p) for p in parts])


def swap(value, axis, shift):
    return lax.ppermute(value, axis, [(i, i ^ shift) for i in range(lax.axis_size(axis))])


def shards(
    queries,
    rerank_queries,
    coarse_book,
    refine_book,
    coarse_codes,
    refine_codes,
    block_place,
    candidates,
):
    holders = lax.axis_size("cells")
    subs = lax.axis_size("sub")
    halves = lax.axis_size("rep")
    own, features = rerank_queries.shape
    rows = queries.reshape(queries.shape[0] // own, own, features)
    book = jnp.swapaxes(coarse_book, 1, 2)
    fine_book = jnp.swapaxes(refine_book, 1, 2).reshape(features, refine_book.shape[1])
    sums = []
    for shift in [*range(1, subs), 0]:
        score = coarse_part(shift, subs, halves, holders, own, rows, book, coarse_codes)
        if shift:
            rows, score = lax.optimization_barrier((rows, score))
            score = swap(score, "sub", shift)
        sums.insert(0 if shift == 0 else len(sums), score)
    fine_codes = [refine_codes.astype(jnp.bfloat16)]
    for k in range(1, holders):
        fine_codes.append(swap(fine_codes[0], "cells", k))
    fine = refine_partials(block_place, candidates.T, rerank_queries, fine_book, fine_codes)
    quarters = list(reduce_subs(halves, sums))
    for r in range(1, halves):
        quarters[r] = swap(quarters[r], "rep", r)
    pieces = combine(quarters)
    got = [pieces[0]]
    for k in range(1, holders):
        got.append(swap(pieces[k], "cells", k))
    fine_parts = pick(subs, block_place, candidates.T, fine, got)
    fine_parts = list(fine_parts)
    for shift in range(1, subs):
        fine_parts[shift] = swap(fine_parts[shift], "sub", shift)
    coarse = arrange(got)
    return coarse, finish(fine_parts)


def solution(mesh):
    placed = (
        P("groups", "sub"),
        P(("groups", "cells", "rep"), "sub"),
        P("sub", None, None),
        P("sub", None, None),
        P("sub", ("groups", "cells")),
        P("sub", ("groups", "cells")),
        P("groups"),
        P(("groups", "cells", "rep"), None),
    )
    return jax.shard_map(
        shards,
        mesh=mesh,
        in_specs=placed,
        out_specs=(
            P(("groups", "cells", "rep"), None, "sub"),
            P(("groups", "cells", "rep"), "sub", None),
        ),
        check_vma=False,
    )
```

```python
from functools import partial

import jax
import jax.numpy as jnp
from jax import lax
from jax.experimental import pallas as pl
from jax.experimental.pallas import tpu as pltpu
from jax.sharding import PartitionSpec as P


BLOCK = 128
LANES = 128

ALONG_LANES = lax.GatherDimensionNumbers(
    offset_dims=(),
    collapsed_slice_dims=(1,),
    start_index_map=(1,),
    operand_batching_dims=(0,),
    start_indices_batching_dims=(0,),
)


def take_lanes(table, index):
    return lax.gather(
        table,
        index[..., None],
        ALONG_LANES,
        (1, 1),
        mode=lax.GatherScatterMode.PROMISE_IN_BOUNDS,
    )


def lookup(table, codes):
    within = codes & (LANES - 1)
    found = take_lanes(table[:, :LANES], within)
    for start in range(LANES, table.shape[1], LANES):
        found = jnp.where(codes >= start, take_lanes(table[:, start : start + LANES], within), found)
    return found


def on_chip(value):
    return pltpu.with_memory_space_constraint(value, pltpu.VMEM)


def lane_group(at):
    return pl.ds(at if isinstance(at, int) else pl.multiple_of(at, LANES), LANES)


def decode(table, codes):
    codes = jnp.broadcast_to(codes.astype(jnp.int16), (table.shape[0], codes.shape[1]))
    within = codes & jnp.int16(LANES - 1)
    found = take_lanes(table[:, :LANES], within)
    for start in range(LANES, table.shape[1], LANES):
        found = jnp.where(
            codes >= jnp.int16(start), take_lanes(table[:, start : start + LANES], within), found
        )
    return found


def coarse_kernel(halves, place, q_ref, book_ref, codes_ref, out_ref):
    spaces, depth, _ = book_ref.shape
    _, own, tiles = out_ref.shape
    holders = out_ref.shape[0] // halves
    half = lax.axis_index("rep")
    rows = jnp.concatenate(
        [
            q_ref[h * halves + (half ^ r)].astype(jnp.float32)
            for r in range(halves)
            for h in range(holders)
        ],
        axis=0,
    ).astype(jnp.bfloat16)
    step = min(spaces, 256 // depth)
    start = place() * tiles if codes_ref.shape[1] > tiles else 0
    for first in range(0, tiles, 2 * LANES):
        scores = None
        for low in range(0, spaces, step):
            decoded = jnp.concatenate(
                [
                    jnp.concatenate(
                        [
                            decode(book_ref[m], codes_ref[m : m + 1, lane_group(start + at)])
                            for at in (first, first + LANES)
                        ],
                        axis=1,
                    )
                    for m in range(low, low + step)
                ],
                axis=0,
            )
            part = jnp.dot(
                rows[:, low * depth : (low + step) * depth],
                decoded,
                preferred_element_type=jnp.float32,
            )
            scores = part if scores is None else scores + part
        for h in range(halves * holders):
            out_ref[h, :, first : first + 2 * LANES] = scores[h * own : (h + 1) * own].astype(
                out_ref.dtype
            )


def coarse_part(shift, subs, halves, holders, own, queries, book, codes):
    spaces, stored = codes.shape
    quarter = stored // subs // halves

    def place():
        return (lax.axis_index("sub") ^ shift) * halves + lax.axis_index("rep")

    whole = pl.BlockSpec(memory_space=pltpu.VMEM)
    block = pl.BlockSpec((spaces, quarter), lambda step: (0, place()))
    operands = (queries, book, codes)
    if shift == 0:
        block, operands = whole, [on_chip(x) for x in operands]
    return pl.pallas_call(
        partial(coarse_kernel, halves, place),
        grid=(1,),
        in_specs=[whole, whole, block],
        out_specs=whole,
        out_shape=pltpu.VMEM(
            (halves * holders, own, quarter), jnp.bfloat16 if shift else jnp.float32
        ),
    )(*operands)


def refine_kernel(holders, subs, place_ref, cand_ref, rerank_ref, book_ref, *refs):
    codes_refs = refs[:holders]
    out_ref, found_ref, wide_ref, table_ref = refs[holders:]
    per_query, own = cand_ref.shape
    spaces, stored = codes_refs[0].shape
    width = book_ref.shape[0]
    depth = width // spaces
    cell_blocks = stored // BLOCK
    part_blocks = cell_blocks // subs
    cell = lax.axis_index("cells")
    sub = lax.axis_index("sub")
    slot = -(-spaces // 8) * 8
    mine = lax.broadcasted_iota(jnp.int32, (slot, width), 1) // depth == (
        lax.broadcasted_iota(jnp.int32, (slot, width), 0)
    )
    rerank = rerank_ref[...].astype(jnp.float32)
    for j in range(own):
        wide_ref[j * slot : (j + 1) * slot, :] = jnp.where(mine, rerank[j : j + 1], 0.0)
    table_ref[...] = jnp.dot(
        wide_ref[...].astype(jnp.bfloat16), book_ref[...], preferred_element_type=jnp.float32
    )
    for j in range(own):
        table = table_ref[j * slot : j * slot + spaces, :]
        for c in range(per_query):
            position = place_ref[cand_ref[c, j]]
            source = lax.div(position, cell_blocks) ^ cell
            block = lax.rem(position, cell_blocks)
            arrival = jnp.where(
                lax.div(block, part_blocks) == sub,
                source * part_blocks + lax.rem(block, part_blocks),
                -1,
            )
            found_ref[j : j + 1, c * BLOCK : (c + 1) * BLOCK] = jnp.full((1, BLOCK), arrival)
            lanes = pl.ds(pl.multiple_of(block * BLOCK, BLOCK), BLOCK)
            codes = codes_refs[0][:, lanes].astype(jnp.float32)
            for k in range(1, holders):
                codes = jnp.where(source == k, codes_refs[k][:, lanes].astype(jnp.float32), codes)
            found = lookup(table, codes.astype(jnp.int32))
            out_ref[j : j + 1, c * BLOCK : (c + 1) * BLOCK] = jnp.sum(found, axis=0, keepdims=True)


def refine_partials(subs, place, cands, reranks, book, codes):
    per_query, own = cands.shape
    spaces = codes[0].shape[0]
    rows = own * (-(-spaces // 8) * 8)
    smem = pl.BlockSpec(memory_space=pltpu.SMEM)
    vmem = pl.BlockSpec(memory_space=pltpu.VMEM)
    return pl.pallas_call(
        partial(refine_kernel, len(codes), subs),
        in_specs=[smem, smem] + [vmem] * (2 + len(codes)),
        out_specs=[vmem, vmem],
        out_shape=[
            pltpu.VMEM((own, per_query * BLOCK), jnp.float32),
            pltpu.VMEM((own, per_query * BLOCK), jnp.int32),
        ],
        scratch_shapes=[
            pltpu.VMEM((rows, book.shape[0]), jnp.float32),
            pltpu.VMEM((rows, book.shape[1]), jnp.float32),
        ],
        name="refine",
    )(place, cands, reranks, book, *[on_chip(c) for c in codes])


def reduce_kernel(halves, *refs):
    in_refs, out_refs = refs[:-halves], refs[-halves:]
    holders = out_refs[0].shape[0]
    for r, out_ref in enumerate(out_refs):
        for h in range(holders):
            total = in_refs[0][r * holders + h]
            for in_ref in in_refs[1:]:
                total = total + in_ref[r * holders + h].astype(jnp.float32)
            out_ref[h] = total.astype(jnp.bfloat16)


def reduce_subs(halves, sums):
    rows, own, quarter = sums[0].shape
    vmem = pl.BlockSpec(memory_space=pltpu.VMEM)
    return pl.pallas_call(
        partial(reduce_kernel, halves),
        in_specs=[vmem] * len(sums),
        out_specs=[vmem] * halves,
        out_shape=[pltpu.VMEM((rows // halves, own, quarter), jnp.bfloat16)] * halves,
        name="reduce",
    )(*[on_chip(s) for s in sums])


def combine_kernel(halves, *refs):
    in_refs, out_refs = refs[:halves], refs[halves:]
    cell = lax.axis_index("cells")
    quarter = in_refs[0].shape[2]
    for k, out_ref in enumerate(out_refs):
        for r, in_ref in enumerate(in_refs):
            at = pl.multiple_of((lax.axis_index("rep") ^ r) * quarter, quarter)
            out_ref[:, pl.ds(at, quarter)] = in_ref[cell ^ k]


def combine(quarters):
    holders, own, quarter = quarters[0].shape
    vmem = pl.BlockSpec(memory_space=pltpu.VMEM)
    return pl.pallas_call(
        partial(combine_kernel, len(quarters)),
        in_specs=[vmem] * len(quarters),
        out_specs=[vmem] * holders,
        out_shape=[pltpu.VMEM((own, quarter * len(quarters)), jnp.bfloat16)] * holders,
        name="combine",
    )(*[on_chip(q) for q in quarters])


def pick_kernel(subs, fine_ref, found_ref, *refs):
    got_refs, out_refs = refs[:-subs], refs[-subs:]
    part_blocks = got_refs[0].shape[1] // BLOCK
    sub = lax.axis_index("sub")
    starts = range(0, fine_ref.shape[1], BLOCK)
    arrivals = [found_ref[:, at : at + BLOCK] for at in starts]
    coarse = [jnp.zeros(arrivals[0].shape, jnp.float32) for _ in starts]
    for k, got_ref in enumerate(got_refs):
        for b in range(part_blocks):
            score = got_ref[:, b * BLOCK : (b + 1) * BLOCK].astype(jnp.float32)
            coarse = [
                jnp.where(arrival == k * part_blocks + b, score, value)
                for arrival, value in zip(arrivals, coarse)
            ]
    sums = [fine_ref[:, at : at + BLOCK] + value for at, value in zip(starts, coarse)]
    each = len(sums) // subs
    for shift, out_ref in enumerate(out_refs):
        for c in range(each):
            value = sums[c]
            for other in range(1, subs):
                value = jnp.where(sub ^ shift == other, sums[other * each + c], value)
            out_ref[:, c * BLOCK : (c + 1) * BLOCK] = value


def pick(subs, fine, found, got):
    own, width = fine.shape
    vmem = pl.BlockSpec(memory_space=pltpu.VMEM)
    return pl.pallas_call(
        partial(pick_kernel, subs),
        in_specs=[vmem] * (2 + len(got)),
        out_specs=[vmem] * subs,
        out_shape=[pltpu.VMEM((own, width // subs), jnp.float32)] * subs,
        name="pick",
    )(on_chip(fine), on_chip(found), *[on_chip(g) for g in got])


def arrange_kernel(*refs):
    in_refs, out_ref, order_ref = refs[:-2], refs[-2], refs[-1]
    cell = lax.axis_index("cells")
    for k, in_ref in enumerate(in_refs):
        order_ref[cell ^ k] = in_ref[...].astype(jnp.float32)
    out_ref[...] = jnp.stack([order_ref[h] for h in range(len(in_refs))], axis=1).astype(
        jnp.bfloat16
    )


def arrange(got):
    holders, (own, part) = len(got), got[0].shape
    return pl.pallas_call(
        arrange_kernel,
        out_shape=jax.ShapeDtypeStruct((own, holders, part), jnp.bfloat16),
        scratch_shapes=[pltpu.VMEM((holders, own, part), jnp.float32)],
        name="arrange",
    )(*[on_chip(g) for g in got])


def finish_kernel(*refs):
    in_refs, out_ref = refs[:-1], refs[-1]
    total = in_refs[0][...]
    for in_ref in in_refs[1:]:
        total = total + in_ref[...]
    out_ref[...] = jnp.stack(
        [total[:, c * BLOCK : (c + 1) * BLOCK] for c in range(out_ref.shape[1])], axis=1
    ).astype(jnp.bfloat16)


def finish(parts):
    own, width = parts[0].shape
    return pl.pallas_call(
        finish_kernel,
        out_shape=jax.ShapeDtypeStruct((own, width // BLOCK, BLOCK), jnp.bfloat16),
        name="finish",
    )(*[on_chip(p) for p in parts])


def swap(value, axis, shift):
    return lax.ppermute(value, axis, [(i, i ^ shift) for i in range(lax.axis_size(axis))])


def shards(
    queries,
    rerank_queries,
    coarse_book,
    refine_book,
    coarse_codes,
    refine_codes,
    block_place,
    candidates,
):
    holders = lax.axis_size("cells")
    subs = lax.axis_size("sub")
    halves = lax.axis_size("rep")
    own, features = rerank_queries.shape
    rows = queries.reshape(queries.shape[0] // own, own, features)
    book = jnp.swapaxes(coarse_book, 1, 2)
    fine_book = jnp.swapaxes(refine_book, 1, 2).reshape(features, refine_book.shape[1])
    sums = []
    for shift in [*range(1, subs), 0]:
        score = coarse_part(shift, subs, halves, holders, own, rows, book, coarse_codes)
        if shift:
            rows, score = lax.optimization_barrier((rows, score))
            score = swap(score, "sub", shift)
        sums.insert(0 if shift == 0 else len(sums), score)
    fine_codes = [refine_codes.astype(jnp.bfloat16)]
    for k in range(1, holders):
        fine_codes.append(swap(fine_codes[0], "cells", k))
    fine, found = refine_partials(
        subs, block_place, candidates.T, rerank_queries, fine_book, fine_codes
    )
    quarters = list(reduce_subs(halves, sums))
    for r in range(1, halves):
        quarters[r] = swap(quarters[r], "rep", r)
    pieces = combine(quarters)
    got = [pieces[0]]
    for k in range(1, holders):
        got.append(swap(pieces[k], "cells", k))
    fine_parts = pick(subs, fine, found, got)
    fine_parts = list(fine_parts)
    for shift in range(1, subs):
        fine_parts[shift] = swap(fine_parts[shift], "sub", shift)
    coarse = arrange(got)
    return coarse, finish(fine_parts)


def solution(mesh):
    placed = (
        P("groups", "sub"),
        P(("groups", "cells", "rep"), "sub"),
        P("sub", None, None),
        P("sub", None, None),
        P("sub", ("groups", "cells")),
        P("sub", ("groups", "cells")),
        P("groups"),
        P(("groups", "cells", "rep"), None),
    )
    return jax.shard_map(
        shards,
        mesh=mesh,
        in_specs=placed,
        out_specs=(
            P(("groups", "cells", "rep"), None, "sub"),
            P(("groups", "cells", "rep"), "sub", None),
        ),
        check_vma=False,
    )
```

```python
from functools import partial

import jax
import jax.numpy as jnp
from jax import lax
from jax.experimental import pallas as pl
from jax.experimental.pallas import tpu as pltpu
from jax.sharding import PartitionSpec as P


BLOCK = 128
LANES = 128

ALONG_LANES = lax.GatherDimensionNumbers(
    offset_dims=(),
    collapsed_slice_dims=(1,),
    start_index_map=(1,),
    operand_batching_dims=(0,),
    start_indices_batching_dims=(0,),
)


def take_lanes(table, index):
    return lax.gather(
        table,
        index[..., None],
        ALONG_LANES,
        (1, 1),
        mode=lax.GatherScatterMode.PROMISE_IN_BOUNDS,
    )


def lookup(table, codes):
    within = codes & (LANES - 1)
    found = take_lanes(table[:, :LANES], within)
    for start in range(LANES, table.shape[1], LANES):
        found = jnp.where(codes >= start, take_lanes(table[:, start : start + LANES], within), found)
    return found


def on_chip(value):
    return pltpu.with_memory_space_constraint(value, pltpu.VMEM)


def lane_group(at):
    return pl.ds(at if isinstance(at, int) else pl.multiple_of(at, LANES), LANES)


def decode(table, codes):
    codes = jnp.broadcast_to(codes.astype(jnp.int16), (table.shape[0], codes.shape[1]))
    within = codes & jnp.int16(LANES - 1)
    found = take_lanes(table[:, :LANES], within)
    for start in range(LANES, table.shape[1], LANES):
        found = jnp.where(
            codes >= jnp.int16(start), take_lanes(table[:, start : start + LANES], within), found
        )
    return found


def coarse_kernel(halves, place, q_ref, book_ref, codes_ref, out_ref, *loads):
    tiles = out_ref.shape[2]
    start = place() * tiles
    chunk = tiles // 4 if tiles % (8 * LANES) == 0 else tiles
    waits = []
    if loads:
        q_load, book_load, codes_load, sems = loads
        copies = [(book_ref, book_load), (q_ref, q_load)] + [
            (
                codes_ref.at[:, pl.ds(pl.multiple_of(start + at, LANES), chunk)],
                codes_load.at[:, at : at + chunk],
            )
            for at in range(0, tiles, chunk)
        ]
        waits = [pltpu.make_async_copy(*pair, sems.at[i]) for i, pair in enumerate(copies)]
        for copy in waits:
            copy.start()
        q_ref, book_ref, codes_ref, start = q_load, book_load, codes_load, 0
        for copy in waits[:2]:
            copy.wait()
        waits = waits[2:]
    spaces, depth, _ = book_ref.shape
    own = out_ref.shape[1]
    holders = out_ref.shape[0] // halves
    half = lax.axis_index("rep")
    rows = jnp.concatenate(
        [
            q_ref[h * halves + (half ^ r)].astype(jnp.float32)
            for r in range(halves)
            for h in range(holders)
        ],
        axis=0,
    ).astype(jnp.bfloat16)
    step = min(spaces, 256 // depth)
    for first in range(0, tiles, 2 * LANES):
        if waits and first % chunk == 0:
            waits.pop(0).wait()
        scores = None
        for low in range(0, spaces, step):
            decoded = jnp.concatenate(
                [
                    jnp.concatenate(
                        [
                            decode(book_ref[m], codes_ref[m : m + 1, lane_group(start + at)])
                            for at in (first, first + LANES)
                        ],
                        axis=1,
                    )
                    for m in range(low, low + step)
                ],
                axis=0,
            )
            part = jnp.dot(
                rows[:, low * depth : (low + step) * depth],
                decoded,
                preferred_element_type=jnp.float32,
            )
            scores = part if scores is None else scores + part
        for h in range(halves * holders):
            out_ref[h, :, first : first + 2 * LANES] = scores[h * own : (h + 1) * own].astype(
                out_ref.dtype
            )


def coarse_part(shift, subs, halves, holders, own, queries, book, codes):
    spaces, stored = codes.shape
    quarter = stored // subs // halves

    def place():
        return (lax.axis_index("sub") ^ shift) * halves + lax.axis_index("rep")

    operands, loads = (queries, book, codes), []
    if shift:
        loads = [pltpu.VMEM(x.shape, x.dtype) for x in (queries, book)]
        loads += [pltpu.VMEM((spaces, quarter), codes.dtype), pltpu.SemaphoreType.DMA((6,))]
    else:
        operands = [on_chip(x) for x in operands]
    return pl.pallas_call(
        partial(coarse_kernel, halves, place),
        in_specs=[pl.BlockSpec(memory_space=pl.ANY if shift else pltpu.VMEM)] * 3,
        out_specs=pl.BlockSpec(memory_space=pltpu.VMEM),
        out_shape=pltpu.VMEM(
            (halves * holders, own, quarter), jnp.bfloat16 if shift else jnp.float32
        ),
        scratch_shapes=loads,
    )(*operands)


def refine_kernel(holders, subs, place_ref, cand_ref, rerank_ref, book_ref, *refs):
    own_ref, codes_refs = refs[0], refs[1:-4]
    out_ref, found_ref, wide_ref, table_ref = refs[-4:]
    halves = len(codes_refs) // (holders - 1)
    per_query, own = cand_ref.shape
    spaces, stored = own_ref.shape
    width = book_ref.shape[0]
    depth = width // spaces
    cell_blocks = stored // BLOCK
    part_blocks = cell_blocks // subs
    cell = lax.axis_index("cells")
    sub = lax.axis_index("sub")
    half = lax.axis_index("rep")
    slot = -(-spaces // 8) * 8
    mine = lax.broadcasted_iota(jnp.int32, (slot, width), 1) // depth == (
        lax.broadcasted_iota(jnp.int32, (slot, width), 0)
    )
    rerank = rerank_ref[...].astype(jnp.float32)
    for j in range(own):
        wide_ref[j * slot : (j + 1) * slot, :] = jnp.where(mine, rerank[j : j + 1], 0.0)
    table_ref[...] = jnp.dot(
        wide_ref[...].astype(jnp.bfloat16), book_ref[...], preferred_element_type=jnp.float32
    )
    for j in range(own):
        table = table_ref[j * slot : j * slot + spaces, :]
        for c in range(per_query):
            position = place_ref[cand_ref[c, j]]
            source = lax.div(position, cell_blocks) ^ cell
            block = lax.rem(position, cell_blocks)
            arrival = jnp.where(
                lax.div(block, part_blocks) == sub,
                source * part_blocks + lax.rem(block, part_blocks),
                -1,
            )
            found_ref[j : j + 1, c * BLOCK : (c + 1) * BLOCK] = jnp.full((1, BLOCK), arrival)
            lanes = pl.ds(pl.multiple_of(block * BLOCK, BLOCK), BLOCK)
            codes = own_ref[:, lanes]
            share = cell_blocks // halves
            lanes = pl.ds(pl.multiple_of(lax.rem(block, share) * BLOCK, BLOCK), BLOCK)
            where = source * halves + (lax.div(block, share) ^ half)
            for at, codes_ref in enumerate(codes_refs, halves):
                got = codes_ref[:, lanes].astype(jnp.float32).astype(jnp.int32)
                codes = jnp.where(where == at, got, codes)
            found = lookup(table, codes)
            out_ref[j : j + 1, c * BLOCK : (c + 1) * BLOCK] = jnp.sum(found, axis=0, keepdims=True)


def refine_partials(holders, subs, place, cands, reranks, book, codes):
    per_query, own = cands.shape
    spaces = codes[0].shape[0]
    rows = own * (-(-spaces // 8) * 8)
    smem = pl.BlockSpec(memory_space=pltpu.SMEM)
    vmem = pl.BlockSpec(memory_space=pltpu.VMEM)
    return pl.pallas_call(
        partial(refine_kernel, holders, subs),
        in_specs=[smem, smem] + [vmem] * (2 + len(codes)),
        out_specs=[vmem, vmem],
        out_shape=[
            pltpu.VMEM((own, per_query * BLOCK), jnp.float32),
            pltpu.VMEM((own, per_query * BLOCK), jnp.int32),
        ],
        scratch_shapes=[
            pltpu.VMEM((rows, book.shape[0]), jnp.float32),
            pltpu.VMEM((rows, book.shape[1]), jnp.float32),
        ],
        name="refine",
    )(place, cands, reranks, book, *[on_chip(c) for c in codes])


def reduce_kernel(halves, *refs):
    in_refs, out_refs = refs[:-halves], refs[-halves:]
    holders = out_refs[0].shape[0]
    for r, out_ref in enumerate(out_refs):
        for h in range(holders):
            total = in_refs[0][r * holders + h]
            for in_ref in in_refs[1:]:
                total = total + in_ref[r * holders + h].astype(jnp.float32)
            out_ref[h] = total.astype(jnp.bfloat16)


def reduce_subs(halves, sums):
    rows, own, quarter = sums[0].shape
    vmem = pl.BlockSpec(memory_space=pltpu.VMEM)
    return pl.pallas_call(
        partial(reduce_kernel, halves),
        in_specs=[vmem] * len(sums),
        out_specs=[vmem] * halves,
        out_shape=[pltpu.VMEM((rows // halves, own, quarter), jnp.bfloat16)] * halves,
        name="reduce",
    )(*[on_chip(s) for s in sums])


def combine_kernel(halves, *refs):
    in_refs, out_refs = refs[:halves], refs[halves:]
    cell = lax.axis_index("cells")
    quarter = in_refs[0].shape[2]
    for k, out_ref in enumerate(out_refs):
        for r, in_ref in enumerate(in_refs):
            at = pl.multiple_of((lax.axis_index("rep") ^ r) * quarter, quarter)
            out_ref[:, pl.ds(at, quarter)] = in_ref[cell ^ k]


def combine(quarters):
    holders, own, quarter = quarters[0].shape
    vmem = pl.BlockSpec(memory_space=pltpu.VMEM)
    return pl.pallas_call(
        partial(combine_kernel, len(quarters)),
        in_specs=[vmem] * len(quarters),
        out_specs=[vmem] * holders,
        out_shape=[pltpu.VMEM((own, quarter * len(quarters)), jnp.bfloat16)] * holders,
        name="combine",
    )(*[on_chip(q) for q in quarters])


def pick_kernel(subs, fine_ref, found_ref, *refs):
    got_refs, out_refs = refs[:-subs], refs[-subs:]
    part_blocks = got_refs[0].shape[1] // BLOCK
    sub = lax.axis_index("sub")
    starts = range(0, fine_ref.shape[1], BLOCK)
    arrivals = [found_ref[:, at : at + BLOCK] for at in starts]
    coarse = [jnp.zeros(arrivals[0].shape, jnp.float32) for _ in starts]
    for k, got_ref in enumerate(got_refs):
        for b in range(part_blocks):
            score = got_ref[:, b * BLOCK : (b + 1) * BLOCK].astype(jnp.float32)
            coarse = [
                jnp.where(arrival == k * part_blocks + b, score, value)
                for arrival, value in zip(arrivals, coarse)
            ]
    sums = [fine_ref[:, at : at + BLOCK] + value for at, value in zip(starts, coarse)]
    each = len(sums) // subs
    for shift, out_ref in enumerate(out_refs):
        for c in range(each):
            value = sums[c]
            for other in range(1, subs):
                value = jnp.where(sub ^ shift == other, sums[other * each + c], value)
            out_ref[:, c * BLOCK : (c + 1) * BLOCK] = value


def pick(subs, fine, found, got):
    own, width = fine.shape
    vmem = pl.BlockSpec(memory_space=pltpu.VMEM)
    return pl.pallas_call(
        partial(pick_kernel, subs),
        in_specs=[vmem] * (2 + len(got)),
        out_specs=[vmem] * subs,
        out_shape=[pltpu.VMEM((own, width // subs), jnp.float32)] * subs,
        name="pick",
    )(on_chip(fine), on_chip(found), *[on_chip(g) for g in got])


def arrange_kernel(*refs):
    in_refs, out_ref, order_ref = refs[:-2], refs[-2], refs[-1]
    cell = lax.axis_index("cells")
    for k, in_ref in enumerate(in_refs):
        order_ref[cell ^ k] = in_ref[...].astype(jnp.float32)
    out_ref[...] = jnp.stack([order_ref[h] for h in range(len(in_refs))], axis=1).astype(
        jnp.bfloat16
    )


def arrange(got):
    holders, (own, part) = len(got), got[0].shape
    return pl.pallas_call(
        arrange_kernel,
        out_shape=jax.ShapeDtypeStruct((own, holders, part), jnp.bfloat16),
        scratch_shapes=[pltpu.VMEM((holders, own, part), jnp.float32)],
        name="arrange",
    )(*[on_chip(g) for g in got])


def finish_kernel(*refs):
    in_refs, out_ref = refs[:-1], refs[-1]
    total = in_refs[0][...]
    for in_ref in in_refs[1:]:
        total = total + in_ref[...]
    out_ref[...] = jnp.stack(
        [total[:, c * BLOCK : (c + 1) * BLOCK] for c in range(out_ref.shape[1])], axis=1
    ).astype(jnp.bfloat16)


def finish(parts):
    own, width = parts[0].shape
    return pl.pallas_call(
        finish_kernel,
        out_shape=jax.ShapeDtypeStruct((own, width // BLOCK, BLOCK), jnp.bfloat16),
        name="finish",
    )(*[on_chip(p) for p in parts])


def swap(value, axis, shift):
    return lax.ppermute(value, axis, [(i, i ^ shift) for i in range(lax.axis_size(axis))])


def shards(
    queries,
    rerank_queries,
    coarse_book,
    refine_book,
    coarse_codes,
    refine_codes,
    block_place,
    candidates,
):
    holders = lax.axis_size("cells")
    subs = lax.axis_size("sub")
    halves = lax.axis_size("rep")
    own, features = rerank_queries.shape
    rows = queries.reshape(queries.shape[0] // own, own, features)
    book = jnp.swapaxes(coarse_book, 1, 2)
    fine_book = jnp.swapaxes(refine_book, 1, 2).reshape(features, refine_book.shape[1])
    sums = []
    for shift in [*range(1, subs), 0]:
        score = coarse_part(shift, subs, halves, holders, own, rows, book, coarse_codes)
        if shift:
            rows, score = lax.optimization_barrier((rows, score))
            score = swap(score, "sub", shift)
        sums.insert(0 if shift == 0 else len(sums), score)
    share = refine_codes.shape[1] // halves
    half_codes = lax.dynamic_slice_in_dim(
        refine_codes, lax.axis_index("rep") * share, share, 1
    ).astype(jnp.bfloat16)
    fine_codes = [refine_codes]
    for k in range(1, holders):
        fine_codes.append(swap(half_codes, "cells", k))
        for r in range(1, halves):
            fine_codes.append(swap(fine_codes[1 + (k - 1) * halves], "rep", r))
    fine, found = refine_partials(
        holders, subs, block_place, candidates.T, rerank_queries, fine_book, fine_codes
    )
    quarters = list(reduce_subs(halves, sums))
    for r in range(1, halves):
        quarters[r] = swap(quarters[r], "rep", r)
    pieces = combine(quarters)
    got = [pieces[0]]
    for k in range(1, holders):
        got.append(swap(pieces[k], "cells", k))
    fine_parts = pick(subs, fine, found, got)
    fine_parts = list(fine_parts)
    for shift in range(1, subs):
        fine_parts[shift] = swap(fine_parts[shift], "sub", shift)
    coarse = arrange(got)
    return coarse, finish(fine_parts)


def solution(mesh):
    placed = (
        P("groups", "sub"),
        P(("groups", "cells", "rep"), "sub"),
        P("sub", None, None),
        P("sub", None, None),
        P("sub", ("groups", "cells")),
        P("sub", ("groups", "cells")),
        P("groups"),
        P(("groups", "cells", "rep"), None),
    )
    return jax.shard_map(
        shards,
        mesh=mesh,
        in_specs=placed,
        out_specs=(
            P(("groups", "cells", "rep"), None, "sub"),
            P(("groups", "cells", "rep"), "sub", None),
        ),
        check_vma=False,
    )
```

```python
from functools import partial

import jax
import jax.numpy as jnp
from jax import lax
from jax.experimental import pallas as pl
from jax.experimental.pallas import tpu as pltpu
from jax.sharding import PartitionSpec as P


BLOCK = 128
LANES = 128

ALONG_LANES = lax.GatherDimensionNumbers(
    offset_dims=(),
    collapsed_slice_dims=(1,),
    start_index_map=(1,),
    operand_batching_dims=(0,),
    start_indices_batching_dims=(0,),
)


def take_lanes(table, index):
    return lax.gather(
        table,
        index[..., None],
        ALONG_LANES,
        (1, 1),
        mode=lax.GatherScatterMode.PROMISE_IN_BOUNDS,
    )


def lookup(table, codes):
    within = codes & (LANES - 1)
    found = take_lanes(table[:, :LANES], within)
    for start in range(LANES, table.shape[1], LANES):
        found = jnp.where(codes >= start, take_lanes(table[:, start : start + LANES], within), found)
    return found


def on_chip(value):
    return pltpu.with_memory_space_constraint(value, pltpu.VMEM)


def decode(table, codes):
    codes = jnp.broadcast_to(codes.astype(jnp.int16), (table.shape[0], codes.shape[1]))
    within = codes & jnp.int16(LANES - 1)
    found = take_lanes(table[:, :LANES], within)
    for start in range(LANES, table.shape[1], LANES):
        found = jnp.where(
            codes >= jnp.int16(start), take_lanes(table[:, start : start + LANES], within), found
        )
    return found


def coarse_kernel(halves, shifts, q_ref, book_ref, codes_ref, out_ref, *loads):
    tiles = out_ref.shape[2]
    chunk = tiles // 4 if tiles % (8 * LANES) == 0 else tiles
    waits, later = [], []
    if loads:
        q_load, book_load, *later_loads, codes_load, sems = loads

        def quarter(shift, at, size):
            place = (lax.axis_index("sub") ^ shift) * halves + lax.axis_index("rep")
            return codes_ref.at[:, pl.ds(pl.multiple_of(place * tiles + at, LANES), size)]

        pairs = [(book_ref, book_load), (q_ref, q_load)]
        for at in range(0, tiles, chunk):
            pairs.append((quarter(shifts[0], at, chunk), codes_load.at[:, at : at + chunk]))
        for shift, load in zip(shifts[1:], later_loads):
            pairs.append((quarter(shift, 0, tiles), load))
        copies = [pltpu.make_async_copy(*pair, sems.at[i]) for i, pair in enumerate(pairs)]
        for copy in copies:
            copy.start()
        q_ref, book_ref, codes_ref = q_load, book_load, codes_load
        for copy in copies[:2]:
            copy.wait()
        waits, later = copies[2 : 2 + tiles // chunk], copies[2 + tiles // chunk :]
    spaces, depth, _ = book_ref.shape
    own = out_ref.shape[1]
    holders = out_ref.shape[0] // halves
    half = lax.axis_index("rep")
    rows = jnp.concatenate(
        [
            q_ref[h * halves + (half ^ r)].astype(jnp.float32)
            for r in range(halves)
            for h in range(holders)
        ],
        axis=0,
    ).astype(jnp.bfloat16)
    step = min(spaces, 256 // depth)
    for first in range(0, tiles, 2 * LANES):
        if waits and first % chunk == 0:
            waits.pop(0).wait()
        scores = None
        for low in range(0, spaces, step):
            decoded = jnp.concatenate(
                [
                    jnp.concatenate(
                        [
                            decode(book_ref[m], codes_ref[m : m + 1, at : at + LANES])
                            for at in (first, first + LANES)
                        ],
                        axis=1,
                    )
                    for m in range(low, low + step)
                ],
                axis=0,
            )
            part = jnp.dot(
                rows[:, low * depth : (low + step) * depth],
                decoded,
                preferred_element_type=jnp.float32,
            )
            scores = part if scores is None else scores + part
        for h in range(halves * holders):
            out_ref[h, :, first : first + 2 * LANES] = scores[h * own : (h + 1) * own].astype(
                out_ref.dtype
            )


    for copy in later:
        copy.wait()


def coarse_first(shifts, subs, halves, holders, own, queries, book, codes):
    spaces, stored = codes.shape
    quarter = stored // subs // halves
    kind = jnp.bfloat16 if shifts[0] else jnp.float32
    load = pltpu.VMEM((spaces, quarter), codes.dtype)
    score, queries, book, *rest = pl.pallas_call(
        partial(coarse_kernel, halves, shifts),
        in_specs=[pl.BlockSpec(memory_space=pl.ANY)] * 3,
        out_specs=[pl.BlockSpec(memory_space=pltpu.VMEM)] * (2 + len(shifts)),
        out_shape=[
            pltpu.VMEM((halves * holders, own, quarter), kind),
            pltpu.VMEM(queries.shape, queries.dtype),
            pltpu.VMEM(book.shape, book.dtype),
        ]
        + [load] * (len(shifts) - 1),
        scratch_shapes=[load, pltpu.SemaphoreType.DMA((5 + len(shifts),))],
        name="coarse_first",
    )(queries, book, codes)
    return score, queries, book, rest


def coarse_next(shift, halves, holders, own, queries, book, codes):
    kind = jnp.bfloat16 if shift else jnp.float32
    vmem = pl.BlockSpec(memory_space=pltpu.VMEM)
    return pl.pallas_call(
        partial(coarse_kernel, halves, (shift,)),
        in_specs=[vmem] * 3,
        out_specs=vmem,
        out_shape=pltpu.VMEM((halves * holders, own, codes.shape[1]), kind),
    )(*[on_chip(x) for x in (queries, book, codes)])


def refine_kernel(holders, subs, place_ref, cand_ref, rerank_ref, book_ref, *refs):
    own_ref, codes_refs = refs[0], refs[1:-4]
    out_ref, found_ref, wide_ref, table_ref = refs[-4:]
    halves = len(codes_refs) // (holders - 1)
    per_query, own = cand_ref.shape
    spaces, stored = own_ref.shape
    width = book_ref.shape[0]
    depth = width // spaces
    cell_blocks = stored // BLOCK
    part_blocks = cell_blocks // subs
    cell = lax.axis_index("cells")
    sub = lax.axis_index("sub")
    half = lax.axis_index("rep")
    slot = -(-spaces // 8) * 8
    mine = lax.broadcasted_iota(jnp.int32, (slot, width), 1) // depth == (
        lax.broadcasted_iota(jnp.int32, (slot, width), 0)
    )
    rerank = rerank_ref[...].astype(jnp.float32)
    for j in range(own):
        wide_ref[j * slot : (j + 1) * slot, :] = jnp.where(mine, rerank[j : j + 1], 0.0)
    table_ref[...] = jnp.dot(
        wide_ref[...].astype(jnp.bfloat16), book_ref[...], preferred_element_type=jnp.float32
    )
    for j in range(own):
        table = table_ref[j * slot : j * slot + spaces, :]
        for c in range(per_query):
            position = place_ref[cand_ref[c, j]]
            source = lax.div(position, cell_blocks) ^ cell
            block = lax.rem(position, cell_blocks)
            arrival = jnp.where(
                lax.div(block, part_blocks) == sub,
                source * part_blocks + lax.rem(block, part_blocks),
                -1,
            )
            found_ref[j : j + 1, c * BLOCK : (c + 1) * BLOCK] = jnp.full((1, BLOCK), arrival)
            lanes = pl.ds(pl.multiple_of(block * BLOCK, BLOCK), BLOCK)
            codes = own_ref[:, lanes]
            share = cell_blocks // halves
            lanes = pl.ds(pl.multiple_of(lax.rem(block, share) * BLOCK, BLOCK), BLOCK)
            where = source * halves + (lax.div(block, share) ^ half)
            for at, codes_ref in enumerate(codes_refs, halves):
                got = codes_ref[:, lanes].astype(jnp.float32).astype(jnp.int32)
                codes = jnp.where(where == at, got, codes)
            found = lookup(table, codes)
            out_ref[j : j + 1, c * BLOCK : (c + 1) * BLOCK] = jnp.sum(found, axis=0, keepdims=True)


def refine_partials(holders, subs, place, cands, reranks, book, codes):
    per_query, own = cands.shape
    spaces = codes[0].shape[0]
    rows = own * (-(-spaces // 8) * 8)
    smem = pl.BlockSpec(memory_space=pltpu.SMEM)
    vmem = pl.BlockSpec(memory_space=pltpu.VMEM)
    return pl.pallas_call(
        partial(refine_kernel, holders, subs),
        in_specs=[smem, smem] + [vmem] * (2 + len(codes)),
        out_specs=[vmem, vmem],
        out_shape=[
            pltpu.VMEM((own, per_query * BLOCK), jnp.float32),
            pltpu.VMEM((own, per_query * BLOCK), jnp.int32),
        ],
        scratch_shapes=[
            pltpu.VMEM((rows, book.shape[0]), jnp.float32),
            pltpu.VMEM((rows, book.shape[1]), jnp.float32),
        ],
        name="refine",
    )(place, cands, *[on_chip(x) for x in (reranks, book, *codes)])


def reduce_kernel(halves, *refs):
    in_refs, out_refs = refs[:-halves], refs[-halves:]
    holders = out_refs[0].shape[0]
    for r, out_ref in enumerate(out_refs):
        for h in range(holders):
            total = in_refs[0][r * holders + h]
            for in_ref in in_refs[1:]:
                total = total + in_ref[r * holders + h].astype(jnp.float32)
            out_ref[h] = total.astype(jnp.bfloat16)


def reduce_subs(halves, sums):
    rows, own, quarter = sums[0].shape
    vmem = pl.BlockSpec(memory_space=pltpu.VMEM)
    return pl.pallas_call(
        partial(reduce_kernel, halves),
        in_specs=[vmem] * len(sums),
        out_specs=[vmem] * halves,
        out_shape=[pltpu.VMEM((rows // halves, own, quarter), jnp.bfloat16)] * halves,
        name="reduce",
    )(*[on_chip(s) for s in sums])


def combine_kernel(halves, *refs):
    in_refs, out_refs = refs[:halves], refs[halves:]
    cell = lax.axis_index("cells")
    quarter = in_refs[0].shape[2]
    for k, out_ref in enumerate(out_refs):
        for r, in_ref in enumerate(in_refs):
            at = pl.multiple_of((lax.axis_index("rep") ^ r) * quarter, quarter)
            out_ref[:, pl.ds(at, quarter)] = in_ref[cell ^ k]


def combine(quarters):
    holders, own, quarter = quarters[0].shape
    vmem = pl.BlockSpec(memory_space=pltpu.VMEM)
    return pl.pallas_call(
        partial(combine_kernel, len(quarters)),
        in_specs=[vmem] * len(quarters),
        out_specs=[vmem] * holders,
        out_shape=[pltpu.VMEM((own, quarter * len(quarters)), jnp.bfloat16)] * holders,
        name="combine",
    )(*[on_chip(q) for q in quarters])


def pick_kernel(subs, fine_ref, found_ref, *refs):
    got_refs, out_refs = refs[:-subs], refs[-subs:]
    part_blocks = got_refs[0].shape[1] // BLOCK
    sub = lax.axis_index("sub")
    starts = range(0, fine_ref.shape[1], BLOCK)
    arrivals = [found_ref[:, at : at + BLOCK] for at in starts]
    coarse = [jnp.zeros(arrivals[0].shape, jnp.float32) for _ in starts]
    for k, got_ref in enumerate(got_refs):
        for b in range(part_blocks):
            score = got_ref[:, b * BLOCK : (b + 1) * BLOCK].astype(jnp.float32)
            coarse = [
                jnp.where(arrival == k * part_blocks + b, score, value)
                for arrival, value in zip(arrivals, coarse)
            ]
    sums = [fine_ref[:, at : at + BLOCK] + value for at, value in zip(starts, coarse)]
    each = len(sums) // subs
    for shift, out_ref in enumerate(out_refs):
        for c in range(each):
            value = sums[c]
            for other in range(1, subs):
                value = jnp.where(sub ^ shift == other, sums[other * each + c], value)
            out_ref[:, c * BLOCK : (c + 1) * BLOCK] = value


def pick(subs, fine, found, got):
    own, width = fine.shape
    vmem = pl.BlockSpec(memory_space=pltpu.VMEM)
    return pl.pallas_call(
        partial(pick_kernel, subs),
        in_specs=[vmem] * (2 + len(got)),
        out_specs=[vmem] * subs,
        out_shape=[pltpu.VMEM((own, width // subs), jnp.float32)] * subs,
        name="pick",
    )(on_chip(fine), on_chip(found), *[on_chip(g) for g in got])


def arrange_kernel(*refs):
    in_refs, out_ref, order_ref = refs[:-2], refs[-2], refs[-1]
    cell = lax.axis_index("cells")
    for k, in_ref in enumerate(in_refs):
        order_ref[cell ^ k] = in_ref[...].astype(jnp.float32)
    out_ref[...] = jnp.stack([order_ref[h] for h in range(len(in_refs))], axis=1).astype(
        jnp.bfloat16
    )


def arrange(got):
    holders, (own, part) = len(got), got[0].shape
    return pl.pallas_call(
        arrange_kernel,
        out_shape=jax.ShapeDtypeStruct((own, holders, part), jnp.bfloat16),
        scratch_shapes=[pltpu.VMEM((holders, own, part), jnp.float32)],
        name="arrange",
    )(*[on_chip(g) for g in got])


def finish_kernel(*refs):
    in_refs, out_ref = refs[:-1], refs[-1]
    total = in_refs[0][...]
    for in_ref in in_refs[1:]:
        total = total + in_ref[...]
    out_ref[...] = jnp.stack(
        [total[:, c * BLOCK : (c + 1) * BLOCK] for c in range(out_ref.shape[1])], axis=1
    ).astype(jnp.bfloat16)


def finish(parts):
    own, width = parts[0].shape
    return pl.pallas_call(
        finish_kernel,
        out_shape=jax.ShapeDtypeStruct((own, width // BLOCK, BLOCK), jnp.bfloat16),
        name="finish",
    )(*[on_chip(p) for p in parts])


def swap(value, axis, shift):
    return lax.ppermute(value, axis, [(i, i ^ shift) for i in range(lax.axis_size(axis))])


def shards(
    queries,
    rerank_queries,
    coarse_book,
    refine_book,
    coarse_codes,
    refine_codes,
    block_place,
    candidates,
):
    holders = lax.axis_size("cells")
    subs = lax.axis_size("sub")
    halves = lax.axis_size("rep")
    own, features = rerank_queries.shape
    rows = queries.reshape(queries.shape[0] // own, own, features)
    book = jnp.swapaxes(coarse_book, 1, 2)
    fine_book = jnp.swapaxes(refine_book, 1, 2).reshape(features, refine_book.shape[1])
    shifts = [*range(1, subs), 0]
    score, rows, book, rest = coarse_first(
        shifts, subs, halves, holders, own, rows, book, coarse_codes
    )
    sums = []
    for at, shift in enumerate(shifts):
        if at:
            score = coarse_next(shift, halves, holders, own, rows, book, rest[at - 1])
        if shift:
            score = swap(score, "sub", shift)
        sums.insert(0 if shift == 0 else len(sums), score)
    share = refine_codes.shape[1] // halves
    half_codes = lax.dynamic_slice_in_dim(
        refine_codes, lax.axis_index("rep") * share, share, 1
    ).astype(jnp.bfloat16)
    fine_codes = [refine_codes]
    for k in range(1, holders):
        fine_codes.append(swap(half_codes, "cells", k))
        for r in range(1, halves):
            fine_codes.append(swap(fine_codes[1 + (k - 1) * halves], "rep", r))
    fine, found = refine_partials(
        holders, subs, block_place, candidates.T, rerank_queries, fine_book, fine_codes
    )
    quarters = list(reduce_subs(halves, sums))
    for r in range(1, halves):
        quarters[r] = swap(quarters[r], "rep", r)
    pieces = combine(quarters)
    got = [pieces[0]]
    for k in range(1, holders):
        got.append(swap(pieces[k], "cells", k))
    fine_parts = pick(subs, fine, found, got)
    fine_parts = list(fine_parts)
    for shift in range(1, subs):
        fine_parts[shift] = swap(fine_parts[shift], "sub", shift)
    coarse = arrange(got)
    return coarse, finish(fine_parts)


def solution(mesh):
    placed = (
        P("groups", "sub"),
        P(("groups", "cells", "rep"), "sub"),
        P("sub", None, None),
        P("sub", None, None),
        P("sub", ("groups", "cells")),
        P("sub", ("groups", "cells")),
        P("groups"),
        P(("groups", "cells", "rep"), None),
    )
    return jax.shard_map(
        shards,
        mesh=mesh,
        in_specs=placed,
        out_specs=(
            P(("groups", "cells", "rep"), None, "sub"),
            P(("groups", "cells", "rep"), "sub", None),
        ),
        check_vma=False,
    )
```

```python
from functools import partial

import jax
import jax.numpy as jnp
from jax import lax
from jax.experimental import pallas as pl
from jax.experimental.pallas import tpu as pltpu
from jax.sharding import PartitionSpec as P


BLOCK = 128
LANES = 128

ALONG_LANES = lax.GatherDimensionNumbers(
    offset_dims=(),
    collapsed_slice_dims=(1,),
    start_index_map=(1,),
    operand_batching_dims=(0,),
    start_indices_batching_dims=(0,),
)


def take_lanes(table, index):
    return lax.gather(
        table,
        index[..., None],
        ALONG_LANES,
        (1, 1),
        mode=lax.GatherScatterMode.PROMISE_IN_BOUNDS,
    )


def lookup(table, codes):
    within = codes & (LANES - 1)
    found = take_lanes(table[:, :LANES], within)
    for start in range(LANES, table.shape[1], LANES):
        found = jnp.where(codes >= start, take_lanes(table[:, start : start + LANES], within), found)
    return found


def on_chip(value):
    return pltpu.with_memory_space_constraint(value, pltpu.VMEM)


def decode(table, codes):
    codes = jnp.broadcast_to(codes.astype(jnp.int16), (table.shape[0], codes.shape[1]))
    within = codes & jnp.int16(LANES - 1)
    found = take_lanes(table[:, :LANES], within)
    for start in range(LANES, table.shape[1], LANES):
        found = jnp.where(
            codes >= jnp.int16(start), take_lanes(table[:, start : start + LANES], within), found
        )
    return found


def coarse_kernel(halves, shifts, q_ref, book_ref, codes_ref, out_ref, *loads):
    tiles = out_ref.shape[2]
    later = []
    if loads:
        q_load, book_load, *later_loads, codes_load, sems = loads

        pairs = [(book_ref, book_load), (q_ref, q_load)]
        for shift, load in zip(shifts, (codes_load, *later_loads)):
            place = (lax.axis_index("sub") ^ shift) * halves + lax.axis_index("rep")
            start = pl.multiple_of(place * tiles, LANES)
            pairs.append((codes_ref.at[:, pl.ds(start, tiles)], load))
        copies = [pltpu.make_async_copy(*pair, sems.at[i]) for i, pair in enumerate(pairs)]
        for copy in copies:
            copy.start()
        q_ref, book_ref, codes_ref = q_load, book_load, codes_load
        for copy in copies[:3]:
            copy.wait()
        later = copies[3:]
    spaces, depth, _ = book_ref.shape
    own = out_ref.shape[1]
    holders = out_ref.shape[0] // halves
    half = lax.axis_index("rep")
    rows = jnp.concatenate(
        [
            q_ref[h * halves + (half ^ r)].astype(jnp.float32)
            for r in range(halves)
            for h in range(holders)
        ],
        axis=0,
    ).astype(jnp.bfloat16)
    step = min(spaces, 256 // depth)
    for first in range(0, tiles, 2 * LANES):
        scores = None
        for low in range(0, spaces, step):
            decoded = jnp.concatenate(
                [
                    jnp.concatenate(
                        [
                            decode(book_ref[m], codes_ref[m : m + 1, at : at + LANES])
                            for at in (first, first + LANES)
                        ],
                        axis=1,
                    )
                    for m in range(low, low + step)
                ],
                axis=0,
            )
            part = jnp.dot(
                rows[:, low * depth : (low + step) * depth],
                decoded,
                preferred_element_type=jnp.float32,
            )
            scores = part if scores is None else scores + part
        for h in range(halves * holders):
            out_ref[h, :, first : first + 2 * LANES] = scores[h * own : (h + 1) * own].astype(
                out_ref.dtype
            )


    for copy in later:
        copy.wait()


def coarse_first(shifts, subs, halves, holders, own, queries, book, codes):
    spaces, stored = codes.shape
    quarter = stored // subs // halves
    kind = jnp.bfloat16 if shifts[0] else jnp.float32
    load = pltpu.VMEM((spaces, quarter), codes.dtype)
    score, queries, book, *rest = pl.pallas_call(
        partial(coarse_kernel, halves, shifts),
        in_specs=[pl.BlockSpec(memory_space=pl.ANY)] * 3,
        out_specs=[pl.BlockSpec(memory_space=pltpu.VMEM)] * (2 + len(shifts)),
        out_shape=[
            pltpu.VMEM((halves * holders, own, quarter), kind),
            pltpu.VMEM(queries.shape, queries.dtype),
            pltpu.VMEM(book.shape, book.dtype),
        ]
        + [load] * (len(shifts) - 1),
        scratch_shapes=[load, pltpu.SemaphoreType.DMA((2 + len(shifts),))],
        name="coarse_first",
    )(queries, book, codes)
    return score, queries, book, rest


def coarse_next(shift, halves, holders, own, queries, book, codes):
    kind = jnp.bfloat16 if shift else jnp.float32
    vmem = pl.BlockSpec(memory_space=pltpu.VMEM)
    return pl.pallas_call(
        partial(coarse_kernel, halves, (shift,)),
        in_specs=[vmem] * 3,
        out_specs=vmem,
        out_shape=pltpu.VMEM((halves * holders, own, codes.shape[1]), kind),
    )(*[on_chip(x) for x in (queries, book, codes)])


def refine_kernel(holders, subs, place_ref, cand_ref, rerank_ref, book_ref, *refs):
    own_ref, codes_refs = refs[0], refs[1:-4]
    out_ref, found_ref, wide_ref, table_ref = refs[-4:]
    halves = len(codes_refs) // (holders - 1)
    per_query, own = cand_ref.shape
    spaces, stored = own_ref.shape
    width = book_ref.shape[0]
    depth = width // spaces
    cell_blocks = stored // BLOCK
    part_blocks = cell_blocks // subs
    cell = lax.axis_index("cells")
    sub = lax.axis_index("sub")
    half = lax.axis_index("rep")
    slot = -(-spaces // 8) * 8
    mine = lax.broadcasted_iota(jnp.int32, (slot, width), 1) // depth == (
        lax.broadcasted_iota(jnp.int32, (slot, width), 0)
    )
    rerank = rerank_ref[...].astype(jnp.float32)
    for j in range(own):
        wide_ref[j * slot : (j + 1) * slot, :] = jnp.where(mine, rerank[j : j + 1], 0.0)
    table_ref[...] = jnp.dot(
        wide_ref[...].astype(jnp.bfloat16), book_ref[...], preferred_element_type=jnp.float32
    )
    for j in range(own):
        table = table_ref[j * slot : j * slot + spaces, :]
        for c in range(per_query):
            position = place_ref[cand_ref[c, j]]
            source = lax.div(position, cell_blocks) ^ cell
            block = lax.rem(position, cell_blocks)
            arrival = jnp.where(
                lax.div(block, part_blocks) == sub,
                source * part_blocks + lax.rem(block, part_blocks),
                -1,
            )
            found_ref[j : j + 1, c * BLOCK : (c + 1) * BLOCK] = jnp.full((1, BLOCK), arrival)
            lanes = pl.ds(pl.multiple_of(block * BLOCK, BLOCK), BLOCK)
            codes = own_ref[:, lanes]
            share = cell_blocks // halves
            lanes = pl.ds(pl.multiple_of(lax.rem(block, share) * BLOCK, BLOCK), BLOCK)
            where = source * halves + (lax.div(block, share) ^ half)
            for at, codes_ref in enumerate(codes_refs, halves):
                got = codes_ref[:, lanes].astype(jnp.float32).astype(jnp.int32)
                codes = jnp.where(where == at, got, codes)
            found = lookup(table, codes)
            out_ref[j : j + 1, c * BLOCK : (c + 1) * BLOCK] = jnp.sum(found, axis=0, keepdims=True)


def refine_partials(holders, subs, place, cands, reranks, book, codes):
    per_query, own = cands.shape
    spaces = codes[0].shape[0]
    rows = own * (-(-spaces // 8) * 8)
    smem = pl.BlockSpec(memory_space=pltpu.SMEM)
    vmem = pl.BlockSpec(memory_space=pltpu.VMEM)
    return pl.pallas_call(
        partial(refine_kernel, holders, subs),
        in_specs=[smem, smem] + [vmem] * (2 + len(codes)),
        out_specs=[vmem, vmem],
        out_shape=[
            pltpu.VMEM((own, per_query * BLOCK), jnp.float32),
            pltpu.VMEM((own, per_query * BLOCK), jnp.int32),
        ],
        scratch_shapes=[
            pltpu.VMEM((rows, book.shape[0]), jnp.float32),
            pltpu.VMEM((rows, book.shape[1]), jnp.float32),
        ],
        name="refine",
    )(place, cands, *[on_chip(x) for x in (reranks, book, *codes)])


def reduce_kernel(halves, *refs):
    in_refs, out_refs = refs[:-halves], refs[-halves:]
    holders = out_refs[0].shape[0]
    for r, out_ref in enumerate(out_refs):
        for h in range(holders):
            total = in_refs[0][r * holders + h]
            for in_ref in in_refs[1:]:
                total = total + in_ref[r * holders + h].astype(jnp.float32)
            out_ref[h] = total.astype(jnp.bfloat16)


def reduce_subs(halves, sums):
    rows, own, quarter = sums[0].shape
    vmem = pl.BlockSpec(memory_space=pltpu.VMEM)
    return pl.pallas_call(
        partial(reduce_kernel, halves),
        in_specs=[vmem] * len(sums),
        out_specs=[vmem] * halves,
        out_shape=[pltpu.VMEM((rows // halves, own, quarter), jnp.bfloat16)] * halves,
        name="reduce",
    )(*[on_chip(s) for s in sums])


def combine_kernel(halves, *refs):
    in_refs, out_refs = refs[:halves], refs[halves:]
    cell = lax.axis_index("cells")
    quarter = in_refs[0].shape[2]
    for k, out_ref in enumerate(out_refs):
        for r, in_ref in enumerate(in_refs):
            at = pl.multiple_of((lax.axis_index("rep") ^ r) * quarter, quarter)
            out_ref[:, pl.ds(at, quarter)] = in_ref[cell ^ k]


def combine(quarters):
    holders, own, quarter = quarters[0].shape
    vmem = pl.BlockSpec(memory_space=pltpu.VMEM)
    return pl.pallas_call(
        partial(combine_kernel, len(quarters)),
        in_specs=[vmem] * len(quarters),
        out_specs=[vmem] * holders,
        out_shape=[pltpu.VMEM((own, quarter * len(quarters)), jnp.bfloat16)] * holders,
        name="combine",
    )(*[on_chip(q) for q in quarters])


def pick_kernel(subs, fine_ref, found_ref, *refs):
    got_refs, out_refs = refs[:-subs], refs[-subs:]
    part_blocks = got_refs[0].shape[1] // BLOCK
    sub = lax.axis_index("sub")
    starts = range(0, fine_ref.shape[1], BLOCK)
    arrivals = [found_ref[:, at : at + BLOCK] for at in starts]
    coarse = [jnp.zeros(arrivals[0].shape, jnp.float32) for _ in starts]
    for k, got_ref in enumerate(got_refs):
        for b in range(part_blocks):
            score = got_ref[:, b * BLOCK : (b + 1) * BLOCK].astype(jnp.float32)
            coarse = [
                jnp.where(arrival == k * part_blocks + b, score, value)
                for arrival, value in zip(arrivals, coarse)
            ]
    sums = [fine_ref[:, at : at + BLOCK] + value for at, value in zip(starts, coarse)]
    each = len(sums) // subs
    for shift, out_ref in enumerate(out_refs):
        for c in range(each):
            value = sums[c]
            for other in range(1, subs):
                value = jnp.where(sub ^ shift == other, sums[other * each + c], value)
            out_ref[:, c * BLOCK : (c + 1) * BLOCK] = value


def pick(subs, fine, found, got):
    own, width = fine.shape
    vmem = pl.BlockSpec(memory_space=pltpu.VMEM)
    return pl.pallas_call(
        partial(pick_kernel, subs),
        in_specs=[vmem] * (2 + len(got)),
        out_specs=[vmem] * subs,
        out_shape=[pltpu.VMEM((own, width // subs), jnp.float32)] * subs,
        name="pick",
    )(on_chip(fine), on_chip(found), *[on_chip(g) for g in got])


def arrange_kernel(*refs):
    in_refs, out_ref, order_ref = refs[:-2], refs[-2], refs[-1]
    cell = lax.axis_index("cells")
    for k, in_ref in enumerate(in_refs):
        order_ref[cell ^ k] = in_ref[...].astype(jnp.float32)
    out_ref[...] = jnp.stack([order_ref[h] for h in range(len(in_refs))], axis=1).astype(
        jnp.bfloat16
    )


def arrange(got):
    holders, (own, part) = len(got), got[0].shape
    return pl.pallas_call(
        arrange_kernel,
        out_shape=jax.ShapeDtypeStruct((own, holders, part), jnp.bfloat16),
        scratch_shapes=[pltpu.VMEM((holders, own, part), jnp.float32)],
        name="arrange",
    )(*[on_chip(g) for g in got])


def finish_kernel(*refs):
    in_refs, out_ref = refs[:-1], refs[-1]
    total = in_refs[0][...]
    for in_ref in in_refs[1:]:
        total = total + in_ref[...]
    out_ref[...] = jnp.stack(
        [total[:, c * BLOCK : (c + 1) * BLOCK] for c in range(out_ref.shape[1])], axis=1
    ).astype(jnp.bfloat16)


def finish(parts):
    own, width = parts[0].shape
    return pl.pallas_call(
        finish_kernel,
        out_shape=jax.ShapeDtypeStruct((own, width // BLOCK, BLOCK), jnp.bfloat16),
        name="finish",
    )(*[on_chip(p) for p in parts])


def swap(value, axis, shift):
    return lax.ppermute(value, axis, [(i, i ^ shift) for i in range(lax.axis_size(axis))])


def shards(
    queries,
    rerank_queries,
    coarse_book,
    refine_book,
    coarse_codes,
    refine_codes,
    block_place,
    candidates,
):
    holders = lax.axis_size("cells")
    subs = lax.axis_size("sub")
    halves = lax.axis_size("rep")
    own, features = rerank_queries.shape
    rows = queries.reshape(queries.shape[0] // own, own, features)
    book = jnp.swapaxes(coarse_book, 1, 2)
    fine_book = jnp.swapaxes(refine_book, 1, 2).reshape(features, refine_book.shape[1])
    shifts = [*range(1, subs), 0]
    score, rows, book, rest = coarse_first(
        shifts, subs, halves, holders, own, rows, book, coarse_codes
    )
    sums = []
    for at, shift in enumerate(shifts):
        if at:
            score = coarse_next(shift, halves, holders, own, rows, book, rest[at - 1])
        if shift:
            score = swap(score, "sub", shift)
        sums.insert(0 if shift == 0 else len(sums), score)
    share = refine_codes.shape[1] // halves
    half_codes = lax.dynamic_slice_in_dim(
        refine_codes, lax.axis_index("rep") * share, share, 1
    ).astype(jnp.bfloat16)
    fine_codes = [refine_codes]
    for k in range(1, holders):
        fine_codes.append(swap(half_codes, "cells", k))
        for r in range(1, halves):
            fine_codes.append(swap(fine_codes[1 + (k - 1) * halves], "rep", r))
    fine, found = refine_partials(
        holders, subs, block_place, candidates.T, rerank_queries, fine_book, fine_codes
    )
    quarters = list(reduce_subs(halves, sums))
    for r in range(1, halves):
        quarters[r] = swap(quarters[r], "rep", r)
    pieces = combine(quarters)
    got = [pieces[0]]
    for k in range(1, holders):
        got.append(swap(pieces[k], "cells", k))
    fine_parts = pick(subs, fine, found, got)
    fine_parts = list(fine_parts)
    for shift in range(1, subs):
        fine_parts[shift] = swap(fine_parts[shift], "sub", shift)
    coarse = arrange(got)
    return coarse, finish(fine_parts)


def solution(mesh):
    placed = (
        P("groups", "sub"),
        P(("groups", "cells", "rep"), "sub"),
        P("sub", None, None),
        P("sub", None, None),
        P("sub", ("groups", "cells")),
        P("sub", ("groups", "cells")),
        P("groups"),
        P(("groups", "cells", "rep"), None),
    )
    return jax.shard_map(
        shards,
        mesh=mesh,
        in_specs=placed,
        out_specs=(
            P(("groups", "cells", "rep"), None, "sub"),
            P(("groups", "cells", "rep"), "sub", None),
        ),
        check_vma=False,
    )
```

```python
from functools import partial

import jax
import jax.numpy as jnp
from jax import lax
from jax.experimental import pallas as pl
from jax.experimental.pallas import tpu as pltpu
from jax.sharding import PartitionSpec as P


BLOCK = 128
LANES = 128

ALONG_LANES = lax.GatherDimensionNumbers(
    offset_dims=(),
    collapsed_slice_dims=(1,),
    start_index_map=(1,),
    operand_batching_dims=(0,),
    start_indices_batching_dims=(0,),
)


def take_lanes(table, index):
    return lax.gather(
        table,
        index[..., None],
        ALONG_LANES,
        (1, 1),
        mode=lax.GatherScatterMode.PROMISE_IN_BOUNDS,
    )


def lookup(table, codes):
    within = codes & (LANES - 1)
    found = take_lanes(table[:, :LANES], within)
    for start in range(LANES, table.shape[1], LANES):
        found = jnp.where(codes >= start, take_lanes(table[:, start : start + LANES], within), found)
    return found


def on_chip(value):
    return pltpu.with_memory_space_constraint(value, pltpu.VMEM)


def decode(table, codes):
    codes = jnp.broadcast_to(codes.astype(jnp.int16), (table.shape[0], codes.shape[1]))
    within = codes & jnp.int16(LANES - 1)
    found = take_lanes(table[:, :LANES], within)
    for start in range(LANES, table.shape[1], LANES):
        found = jnp.where(
            codes >= jnp.int16(start), take_lanes(table[:, start : start + LANES], within), found
        )
    return found


def coarse_kernel(halves, shifts, q_ref, book_ref, codes_ref, *refs):
    first = len(refs) > 1
    out_ref, *loads = refs[1:] if first else refs
    tiles = out_ref.shape[2]
    later = []
    if first:
        q_load, book_load, fine_load, *later_loads, codes_load, sems = loads
        pairs = [(book_ref, book_load), (q_ref, q_load)]
        for shift, load in zip(shifts, (codes_load, *later_loads)):
            place = (lax.axis_index("sub") ^ shift) * halves + lax.axis_index("rep")
            start = pl.multiple_of(place * tiles, LANES)
            pairs.append((codes_ref.at[:, pl.ds(start, tiles)], load))
        pairs.append((refs[0], fine_load))
        copies = [pltpu.make_async_copy(*pair, sems.at[i]) for i, pair in enumerate(pairs)]
        now, later = copies[:3], copies[3:]
        for copy in now:
            copy.start()
        q_ref, book_ref, codes_ref = q_load, book_load, codes_load
        for copy in now:
            copy.wait()
        for copy in later:
            copy.start()
    spaces, depth, _ = book_ref.shape
    own = out_ref.shape[1]
    holders = out_ref.shape[0] // halves
    half = lax.axis_index("rep")
    rows = jnp.concatenate(
        [
            q_ref[h * halves + (half ^ r)].astype(jnp.float32)
            for r in range(halves)
            for h in range(holders)
        ],
        axis=0,
    ).astype(jnp.bfloat16)
    step = min(spaces, 256 // depth)
    for first in range(0, tiles, 2 * LANES):
        scores = None
        for low in range(0, spaces, step):
            decoded = jnp.concatenate(
                [
                    jnp.concatenate(
                        [
                            decode(book_ref[m], codes_ref[m : m + 1, at : at + LANES])
                            for at in (first, first + LANES)
                        ],
                        axis=1,
                    )
                    for m in range(low, low + step)
                ],
                axis=0,
            )
            part = jnp.dot(
                rows[:, low * depth : (low + step) * depth],
                decoded,
                preferred_element_type=jnp.float32,
            )
            scores = part if scores is None else scores + part
        for h in range(halves * holders):
            out_ref[h, :, first : first + 2 * LANES] = scores[h * own : (h + 1) * own].astype(
                out_ref.dtype
            )
    for copy in later:
        copy.wait()


def coarse_first(shifts, subs, halves, holders, own, queries, book, codes, fine_codes):
    spaces, stored = codes.shape
    quarter = stored // subs // halves
    kind = jnp.bfloat16 if shifts[0] else jnp.float32
    load = pltpu.VMEM((spaces, quarter), codes.dtype)
    score, queries, book, fine_codes, *rest = pl.pallas_call(
        partial(coarse_kernel, halves, shifts),
        in_specs=[pl.BlockSpec(memory_space=pl.ANY)] * 4,
        out_specs=[pl.BlockSpec(memory_space=pltpu.VMEM)] * (3 + len(shifts)),
        out_shape=[
            pltpu.VMEM((halves * holders, own, quarter), kind),
            pltpu.VMEM(queries.shape, queries.dtype),
            pltpu.VMEM(book.shape, book.dtype),
            pltpu.VMEM(fine_codes.shape, fine_codes.dtype),
        ]
        + [load] * (len(shifts) - 1),
        scratch_shapes=[load, pltpu.SemaphoreType.DMA((3 + len(shifts),))],
        name="coarse_first",
    )(queries, book, codes, fine_codes)
    return score, queries, book, fine_codes, rest


def coarse_next(shift, halves, holders, own, queries, book, codes):
    kind = jnp.bfloat16 if shift else jnp.float32
    vmem = pl.BlockSpec(memory_space=pltpu.VMEM)
    return pl.pallas_call(
        partial(coarse_kernel, halves, (shift,)),
        in_specs=[vmem] * 3,
        out_specs=vmem,
        out_shape=pltpu.VMEM((halves * holders, own, codes.shape[1]), kind),
    )(*[on_chip(x) for x in (queries, book, codes)])


def refine_kernel(holders, subs, place_ref, cand_ref, rerank_ref, book_ref, *refs):
    own_ref, codes_refs = refs[0], refs[1:-4]
    out_ref, found_ref, wide_ref, table_ref = refs[-4:]
    halves = len(codes_refs) // (holders - 1)
    per_query, own = cand_ref.shape
    spaces, stored = own_ref.shape
    width = book_ref.shape[0]
    depth = width // spaces
    cell_blocks = stored // BLOCK
    part_blocks = cell_blocks // subs
    cell = lax.axis_index("cells")
    sub = lax.axis_index("sub")
    half = lax.axis_index("rep")
    slot = -(-spaces // 8) * 8
    mine = lax.broadcasted_iota(jnp.int32, (slot, width), 1) // depth == (
        lax.broadcasted_iota(jnp.int32, (slot, width), 0)
    )
    rerank = rerank_ref[...].astype(jnp.float32)
    for j in range(own):
        wide_ref[j * slot : (j + 1) * slot, :] = jnp.where(mine, rerank[j : j + 1], 0.0)
    table_ref[...] = jnp.dot(
        wide_ref[...].astype(jnp.bfloat16), book_ref[...], preferred_element_type=jnp.float32
    )
    for j in range(own):
        table = table_ref[j * slot : j * slot + spaces, :]
        for c in range(per_query):
            position = place_ref[cand_ref[c, j]]
            source = lax.div(position, cell_blocks) ^ cell
            block = lax.rem(position, cell_blocks)
            arrival = jnp.where(
                lax.div(block, part_blocks) == sub,
                source * part_blocks + lax.rem(block, part_blocks),
                -1,
            )
            found_ref[j : j + 1, c * BLOCK : (c + 1) * BLOCK] = jnp.full((1, BLOCK), arrival)
            lanes = pl.ds(pl.multiple_of(block * BLOCK, BLOCK), BLOCK)
            codes = own_ref[:, lanes]
            share = cell_blocks // halves
            lanes = pl.ds(pl.multiple_of(lax.rem(block, share) * BLOCK, BLOCK), BLOCK)
            where = source * halves + (lax.div(block, share) ^ half)
            for at, codes_ref in enumerate(codes_refs, halves):
                got = codes_ref[:, lanes].astype(jnp.float32).astype(jnp.int32)
                codes = jnp.where(where == at, got, codes)
            found = lookup(table, codes)
            out_ref[j : j + 1, c * BLOCK : (c + 1) * BLOCK] = jnp.sum(found, axis=0, keepdims=True)


def refine_partials(holders, subs, place, cands, reranks, book, codes):
    per_query, own = cands.shape
    spaces = codes[0].shape[0]
    rows = own * (-(-spaces // 8) * 8)
    smem = pl.BlockSpec(memory_space=pltpu.SMEM)
    vmem = pl.BlockSpec(memory_space=pltpu.VMEM)
    return pl.pallas_call(
        partial(refine_kernel, holders, subs),
        in_specs=[smem, smem] + [vmem] * (2 + len(codes)),
        out_specs=[vmem, vmem],
        out_shape=[
            pltpu.VMEM((own, per_query * BLOCK), jnp.float32),
            pltpu.VMEM((own, per_query * BLOCK), jnp.int32),
        ],
        scratch_shapes=[
            pltpu.VMEM((rows, book.shape[0]), jnp.float32),
            pltpu.VMEM((rows, book.shape[1]), jnp.float32),
        ],
        name="refine",
    )(place, cands, *[on_chip(x) for x in (reranks, book, *codes)])


def reduce_kernel(halves, *refs):
    in_refs, out_refs = refs[:-halves], refs[-halves:]
    holders = out_refs[0].shape[0]
    for r, out_ref in enumerate(out_refs):
        for h in range(holders):
            total = in_refs[0][r * holders + h]
            for in_ref in in_refs[1:]:
                total = total + in_ref[r * holders + h].astype(jnp.float32)
            out_ref[h] = total.astype(jnp.bfloat16)


def reduce_subs(halves, sums):
    rows, own, quarter = sums[0].shape
    vmem = pl.BlockSpec(memory_space=pltpu.VMEM)
    return pl.pallas_call(
        partial(reduce_kernel, halves),
        in_specs=[vmem] * len(sums),
        out_specs=[vmem] * halves,
        out_shape=[pltpu.VMEM((rows // halves, own, quarter), jnp.bfloat16)] * halves,
        name="reduce",
    )(*[on_chip(s) for s in sums])


def combine_kernel(halves, *refs):
    in_refs, out_refs = refs[:halves], refs[halves:]
    cell = lax.axis_index("cells")
    quarter = in_refs[0].shape[2]
    for k, out_ref in enumerate(out_refs):
        for r, in_ref in enumerate(in_refs):
            at = pl.multiple_of((lax.axis_index("rep") ^ r) * quarter, quarter)
            out_ref[:, pl.ds(at, quarter)] = in_ref[cell ^ k]


def combine(quarters):
    holders, own, quarter = quarters[0].shape
    vmem = pl.BlockSpec(memory_space=pltpu.VMEM)
    return pl.pallas_call(
        partial(combine_kernel, len(quarters)),
        in_specs=[vmem] * len(quarters),
        out_specs=[vmem] * holders,
        out_shape=[pltpu.VMEM((own, quarter * len(quarters)), jnp.bfloat16)] * holders,
        name="combine",
    )(*[on_chip(q) for q in quarters])


def pick_kernel(subs, fine_ref, found_ref, *refs):
    got_refs, out_refs = refs[:-subs], refs[-subs:]
    part_blocks = got_refs[0].shape[1] // BLOCK
    sub = lax.axis_index("sub")
    starts = range(0, fine_ref.shape[1], BLOCK)
    arrivals = [found_ref[:, at : at + BLOCK] for at in starts]
    coarse = [jnp.zeros(arrivals[0].shape, jnp.float32) for _ in starts]
    for k, got_ref in enumerate(got_refs):
        for b in range(part_blocks):
            score = got_ref[:, b * BLOCK : (b + 1) * BLOCK].astype(jnp.float32)
            coarse = [
                jnp.where(arrival == k * part_blocks + b, score, value)
                for arrival, value in zip(arrivals, coarse)
            ]
    sums = [fine_ref[:, at : at + BLOCK] + value for at, value in zip(starts, coarse)]
    each = len(sums) // subs
    for shift, out_ref in enumerate(out_refs):
        for c in range(each):
            value = sums[c]
            for other in range(1, subs):
                value = jnp.where(sub ^ shift == other, sums[other * each + c], value)
            out_ref[:, c * BLOCK : (c + 1) * BLOCK] = value


def pick(subs, fine, found, got):
    own, width = fine.shape
    vmem = pl.BlockSpec(memory_space=pltpu.VMEM)
    return pl.pallas_call(
        partial(pick_kernel, subs),
        in_specs=[vmem] * (2 + len(got)),
        out_specs=[vmem] * subs,
        out_shape=[pltpu.VMEM((own, width // subs), jnp.float32)] * subs,
        name="pick",
    )(on_chip(fine), on_chip(found), *[on_chip(g) for g in got])


def arrange_kernel(*refs):
    in_refs, out_ref, order_ref = refs[:-2], refs[-2], refs[-1]
    cell = lax.axis_index("cells")
    for k, in_ref in enumerate(in_refs):
        order_ref[cell ^ k] = in_ref[...].astype(jnp.float32)
    out_ref[...] = jnp.stack([order_ref[h] for h in range(len(in_refs))], axis=1).astype(
        jnp.bfloat16
    )


def arrange(got):
    holders, (own, part) = len(got), got[0].shape
    return pl.pallas_call(
        arrange_kernel,
        out_shape=jax.ShapeDtypeStruct((own, holders, part), jnp.bfloat16),
        scratch_shapes=[pltpu.VMEM((holders, own, part), jnp.float32)],
        name="arrange",
    )(*[on_chip(g) for g in got])


def finish_kernel(*refs):
    in_refs, out_ref = refs[:-1], refs[-1]
    total = in_refs[0][...]
    for in_ref in in_refs[1:]:
        total = total + in_ref[...]
    out_ref[...] = jnp.stack(
        [total[:, c * BLOCK : (c + 1) * BLOCK] for c in range(out_ref.shape[1])], axis=1
    ).astype(jnp.bfloat16)


def finish(parts):
    own, width = parts[0].shape
    return pl.pallas_call(
        finish_kernel,
        out_shape=jax.ShapeDtypeStruct((own, width // BLOCK, BLOCK), jnp.bfloat16),
        name="finish",
    )(*[on_chip(p) for p in parts])


def swap(value, axis, shift):
    return lax.ppermute(value, axis, [(i, i ^ shift) for i in range(lax.axis_size(axis))])


def shards(
    queries,
    rerank_queries,
    coarse_book,
    refine_book,
    coarse_codes,
    refine_codes,
    block_place,
    candidates,
):
    holders = lax.axis_size("cells")
    subs = lax.axis_size("sub")
    halves = lax.axis_size("rep")
    own, features = rerank_queries.shape
    rows = queries.reshape(queries.shape[0] // own, own, features)
    book = jnp.swapaxes(coarse_book, 1, 2)
    fine_book = jnp.swapaxes(refine_book, 1, 2).reshape(features, refine_book.shape[1])
    shifts = [*range(1, subs), 0]
    score, rows, book, refine_codes, rest = coarse_first(
        shifts, subs, halves, holders, own, rows, book, coarse_codes, refine_codes
    )
    sums = []
    for at, shift in enumerate(shifts):
        if at:
            score = coarse_next(shift, halves, holders, own, rows, book, rest[at - 1])
        if shift:
            score = swap(score, "sub", shift)
        sums.insert(0 if shift == 0 else len(sums), score)
    share = refine_codes.shape[1] // halves
    half_codes = lax.dynamic_slice_in_dim(
        refine_codes, lax.axis_index("rep") * share, share, 1
    ).astype(jnp.bfloat16)
    fine_codes = [refine_codes]
    for k in range(1, holders):
        fine_codes.append(swap(half_codes, "cells", k))
        for r in range(1, halves):
            fine_codes.append(swap(fine_codes[1 + (k - 1) * halves], "rep", r))
    fine, found = refine_partials(
        holders, subs, block_place, candidates.T, rerank_queries, fine_book, fine_codes
    )
    quarters = list(reduce_subs(halves, sums))
    for r in range(1, halves):
        quarters[r] = swap(quarters[r], "rep", r)
    pieces = combine(quarters)
    got = [pieces[0]]
    for k in range(1, holders):
        got.append(swap(pieces[k], "cells", k))
    fine_parts = pick(subs, fine, found, got)
    fine_parts = list(fine_parts)
    for shift in range(1, subs):
        fine_parts[shift] = swap(fine_parts[shift], "sub", shift)
    coarse = arrange(got)
    return coarse, finish(fine_parts)


def solution(mesh):
    placed = (
        P("groups", "sub"),
        P(("groups", "cells", "rep"), "sub"),
        P("sub", None, None),
        P("sub", None, None),
        P("sub", ("groups", "cells")),
        P("sub", ("groups", "cells")),
        P("groups"),
        P(("groups", "cells", "rep"), None),
    )
    return jax.shard_map(
        shards,
        mesh=mesh,
        in_specs=placed,
        out_specs=(
            P(("groups", "cells", "rep"), None, "sub"),
            P(("groups", "cells", "rep"), "sub", None),
        ),
        check_vma=False,
    )
```
